128 devices in a mesh: seg: 16 (over y, z), col: 8 (over x, core).
Axes of the slice: x: 4, y: 4, z: 4, core: 2. Of those that a mesh axis runs over, the one named last changes fastest.
Arguments:
- model_mixing: float32 [32, 384, 384], P('seg', 'col'), may hold values from -0.07654656 to 0.07654656
- retention: float32 [32, 384], P('seg'), may hold values from 0.5 to 0.95
- forcing: float32 [32, 384], P('seg'), may hold values from -1.2 to 1.2
- observations: float32 [32, 1024], P('seg'), may hold values from -6 to 6
- model_noise: float32 [32, 384], P('seg'), may hold values from 0.01 to 0.1
- obs_noise: float32 [1024], replicated, may hold values from 0.5 to 2
- gain: float32 [384, 1024], replicated, may hold values from -0.01875 to 0.01875
- obs_operator_t: float32 [384, 1024], P('col'), may hold values from -0.30618623 to 0.30618623
- prior_mean: float32 [384], replicated, may hold values from -6 to 6
- prior_factor: float32 [384, 384], replicated, may hold values from -0.3125 to 0.3125
Outputs:
- means: float32 [32, 384], P('seg')
- covariances: float32 [32, 384, 384], P('seg', 'col')
The draws below stay inside these ranges and needn't reach their ends.
All inputs are finite; a program needn't handle non-finite values.
Results may differ from the reference program's by a relative error of at most 0.00019.
Values sent between devices are 32-bit elements; how exact they have to be, the bound alone decides.
A program may use at most 64 MiB of HBM per device.

```python
import math
import jax
import jax.numpy as jnp
from jax import lax

N = 384
NOBS = 1024
WINDOW = 32


def shard_levels(stream_key, shape, split, low, largest):
    level = 1.0
    for axis_at, shards_of in split:
        heights = jax.random.uniform(jax.random.fold_in(jax.random.fold_in(stream_key, 6), axis_at), (shards_of,), jnp.float32, low / len(split), largest / len(split))
        level = level * jnp.repeat(jnp.exp(heights), shape[axis_at] // shards_of).reshape((-1,) + (1,) * (len(shape) - 1 - axis_at))
    return level


def bell_draw(stream_key, extent, spread, most, shards=(), held_as=jnp.bfloat16):
    drawn = spread * jax.random.normal(stream_key, extent, jnp.float32)
    if shards:
        drawn = drawn * shard_levels(stream_key, extent, shards, -0.22, 0.18)
    return jnp.clip(drawn, -most, most).astype(held_as)


def setup_inputs(seed: int = 0) -> dict:
    key_list = jax.random.split(jax.random.key(seed), 11)
    return {
        "model_mixing": bell_draw(key_list[0], (WINDOW, N, N), (0.25 / N ** 0.5), 0.07654656, ((0, 16), (1, 8)), jnp.float32),
        "retention": jnp.clip(jnp.exp(math.log(0.95) - 0.64185387 * jax.random.uniform(key_list[1], (WINDOW, N), jnp.float32) ** shard_levels(key_list[1], (WINDOW, N), ((0, 16),), -0.2, 0.2)), 0.5, 0.95),
        "forcing": bell_draw(key_list[2], (WINDOW, N), 0.2, 1.2, ((0, 16),), jnp.float32),
        "observations": bell_draw(key_list[3], (WINDOW, NOBS), 1.0, 6.0, ((0, 16),), jnp.float32),
        "model_noise": jnp.clip(jnp.exp(math.log(0.1) - 2.3025851 * jax.random.uniform(key_list[4], (WINDOW, N), jnp.float32) ** shard_levels(key_list[4], (WINDOW, N), ((0, 16),), -0.2, 0.2)), 0.01, 0.1),
        "obs_noise": jnp.clip(jnp.exp(jax.random.uniform(key_list[5], (NOBS,), jnp.float32, math.log(0.5), math.log(2.0))), 0.5, 2.0),
        "gain": bell_draw(key_list[6], (N, NOBS), (0.1 / NOBS ** 0.5), 0.01875, (), jnp.float32),
        "obs_operator_t": bell_draw(key_list[7], (N, NOBS), (1.0 / N ** 0.5), 0.30618623, ((0, 8),), jnp.float32),
        "prior_mean": bell_draw(key_list[8], (N,), 1.0, 6.0, (), jnp.float32),
        "prior_factor": bell_draw(key_list[9], (N, N), N ** -0.5, 0.3125, (), jnp.float32),
    }


precise = lax.Precision.HIGHEST


def product(left, right):
    return jnp.dot(left, right, precision=precise, preferred_element_type=jnp.float32)


def reference(model_mixing, retention, forcing, observations, model_noise, obs_noise, gain, obs_operator_t, prior_mean, prior_factor):
    identity = jnp.eye(N, dtype=jnp.float32)
    correction = identity - product(gain, obs_operator_t.T)
    fixed_noise = product(gain * obs_noise[None, :], gain.T)

    def advance(carried, inputs):
        mean_now, covar_now = carried
        mixing, keeping, pushing, observed, variances = inputs
        model_step = jnp.diag(keeping) + mixing.T
        step_matrix = product(correction, model_step)
        step_offset = product(correction, pushing) + product(gain, observed)
        step_noise = product(correction * variances[None, :], correction.T) + fixed_noise
        mean_next = product(step_matrix, mean_now) + step_offset
        covar_next = product(product(step_matrix, covar_now), step_matrix.T) + step_noise
        return (mean_next, covar_next), (mean_next, covar_next)

    initial = (prior_mean, product(prior_factor, prior_factor.T))
    final_pair, outputs = lax.scan(advance, initial, (model_mixing, retention, forcing, observations, model_noise))
    return outputs[0], outputs[1]
```

```python
import functools

import jax
import jax.numpy as jnp
from jax import lax
from jax.experimental import pallas as pl
from jax.experimental.pallas import tpu as pltpu
from jax.sharding import Mesh
from jax.sharding import PartitionSpec as P

MESH = pl.DeviceIdType.MESH
F32 = jnp.float32
BF16 = jnp.bfloat16
SEG = ("y", "z")
COL = ("x", "c")
N = 384
NOBS = 1024
W = 48
CR = 24
PER_CLASS = 36


def split(value):
    high = value.astype(BF16)
    low = (value - high.astype(F32)).astype(BF16)
    return high, low


def dot(left, right, transposed):
    dims = (((1,), (1 if transposed else 0,)), ((), ()))
    return lax.dot_general(left, right, dims, preferred_element_type=F32)


def product(left, right_high, right_low, transposed=False):
    high, low = split(left)
    rows = left.shape[0]
    both = dot(jnp.concatenate([high, low], 0), right_high, transposed)
    return both[:rows] + (both[rows:] + dot(high, right_low, transposed))


def put_split(high_ref, low_ref, index, value):
    high, low = split(value)
    high_ref[index] = high
    low_ref[index] = low


def turn(position, by):
    return lax.rem(position + (by % 4), 4)


class PlaneGather:
    def __init__(self, unit, rows, core, first, second, to_first, to_second, partner, send, recv, base, sent):
        self.unit, self.rows, self.core = unit, rows, core
        self.f = [turn(first, d) for d in (0, -1, 1, 2)]
        self.s = [turn(second, d) for d in (0, -1, 1, 2)]
        self.to_first, self.to_second, self.partner = to_first, to_second, partner
        self.send, self.recv, self.base, self.sent = send, recv, base, sent

    def at(self, kf, ks, half=None, core=None):
        ref = self.unit(self.core if core is None else core, self.f[kf], self.s[ks])
        if half is None:
            return ref
        middle = self.rows // 2
        return ref.at[pl.ds(half * middle, middle)]

    def start(self, index, source, target, device):
        copy = pltpu.make_async_remote_copy(
            src_ref=source,
            dst_ref=target,
            send_sem=self.send.at[self.base + index],
            recv_sem=self.recv.at[self.base + index],
            device_id=device,
            device_id_type=MESH,
        )
        copy.start()
        self.sent.append(copy)

    def arrive(self, index, slot):
        pltpu.make_async_remote_copy(
            src_ref=slot,
            dst_ref=slot,
            send_sem=self.send.at[self.base + index],
            recv_sem=self.recv.at[self.base + index],
            device_id=self.partner,
            device_id_type=MESH,
        ).wait_recv()

    def first_own(self, source):
        for way in (0, 1):
            self.start(way, source, self.at(0, 0), self.to_first[way])

    def share(self, kf, ks, source=None):
        slot = self.at(kf, ks)
        self.start(20 + 4 * ks + kf, slot if source is None else source, slot, self.partner)

    def shared(self, kf, ks):
        self.arrive(20 + 4 * ks + kf, self.at(kf, ks, core=1 - self.core))

    def second(self, kf, source=None):
        slot = self.at(kf, 0)
        for way in (0, 1):
            self.start(4 + 2 * kf + way, slot if source is None else source, slot, self.to_second[way])

    def first_near(self):
        for way in (0, 1):
            self.arrive(way, self.at(1 + way, 0))
            part = self.at(1 + way, 0, half=way)
            self.start(2 + way, part, part, self.to_first[way])
            self.second(1 + way)
            self.share(1 + way, 0)

    def first_far(self):
        for way in (0, 1):
            self.arrive(2 + way, self.at(3, 0, half=way))
        self.second(3)
        self.share(3, 0)

    def second_near(self, kf):
        for way in (0, 1):
            self.arrive(4 + 2 * kf + way, self.at(kf, 1 + way))
            part = self.at(kf, 1 + way, half=way)
            self.start(12 + 2 * kf + way, part, part, self.to_second[way])
            self.share(kf, 1 + way)

    def second_far(self, kf):
        for way in (0, 1):
            self.arrive(12 + 2 * kf + way, self.at(kf, 3, half=way))
        self.share(kf, 3)


def kernel(
    mixing, retention, forcing, observations, model_noise, obs_noise, gain, obs_t, prior_mean, prior_factor,
    means, covariances,
    ga, gb, cg, ea, eb, ret4, forc4, obs4, noise4, ret8, forc16, obs16, noise8, on_v, gain_v, gain_h, gain_l,
    obs_v, pm_v, pf_v, ct_h, ct_l, fix_h, fix_l, p_h, p_l, b_h, b_l, off8, wc, gc, wf, gf, stage, stage_mean,
    near_mean, t1_h, t1_l, n1_h, n1_l, t2_h, t2_l, n2_h, n2_l, w0_s, v1_s, v2_s, xs,
    send1, recv1, send3, recv3, send_c, recv_c, send_s, recv_s, send_y, recv_y, local,
):
    y, z, x, c = (lax.axis_index(name) for name in ("y", "z", "x", "c"))
    partner = (y, z, x, 1 - c)
    x_to = [(y, z, turn(x, 1), c), (y, z, turn(x, -1), c)]
    z_to = [(y, turn(z, 1), x, c), (y, turn(z, -1), x, c)]
    x_far, z_far = (y, z, turn(x, 2), c), (y, turn(z, 2), x, c)
    y_to = [(turn(y, d), z, x, c) for d in (1, 2, 3)]
    sent = []

    own = {}
    for index, (name, source, target) in enumerate(
        (
            ("gain", gain, gain_v),
            ("obs_t", obs_t, obs_v),
            ("mix0", mixing.at[0], ga.at[c, z, x]),
            ("mix1", mixing.at[1], gb.at[c, x, z]),
            ("noise", obs_noise, on_v),
            ("ret", retention, ret4.at[z]),
            ("forc", forcing, forc4.at[z]),
            ("obs", observations, obs4.at[z]),
            ("mn", model_noise, noise4.at[z]),
            ("pm", prior_mean, pm_v),
            ("pf", prior_factor, pf_v),
        )
    ):
        own[name] = pltpu.make_async_copy(source, target, local.at[index])
        own[name].start()

    ea[c, z, x] = jnp.zeros((32, N), F32)
    eb[c, x, z] = jnp.zeros((32, N), F32)
    forc16[...] = jnp.zeros((16, N), F32)
    obs16[...] = jnp.zeros((16, NOBS), F32)

    barrier = pltpu.get_barrier_semaphore()
    friends = [partner] + x_to + [x_far] + z_to + [z_far] + y_to
    for friend in friends:
        pl.semaphore_signal(barrier, inc=1, device_id=friend, device_id_type=MESH)
    pl.semaphore_wait(barrier, len(friends))

    first = PlaneGather(lambda core, f, s: ga.at[core, s, f], W, c, x, z, x_to, z_to, partner, send1, recv1, 0, sent)
    other = PlaneGather(
        lambda core, f, s: gb.at[core, s, f], W, c, z, x, z_to, x_to, partner, send1, recv1, PER_CLASS, sent
    )
    first.first_own(mixing.at[0])
    other.first_own(mixing.at[1])
    first.second(0, mixing.at[0])
    first.share(0, 0, mixing.at[0])
    other.share(0, 0, mixing.at[1])

    small = []
    for array, (source, target) in enumerate(
        ((retention, ret4), (forcing, forc4), (observations, obs4), (model_noise, noise4))
    ):
        for d in (1, 2, 3):
            index = 3 * array + d - 1
            copy = pltpu.make_async_remote_copy(
                src_ref=source,
                dst_ref=target.at[z],
                send_sem=send_s.at[index],
                recv_sem=recv_s.at[index],
                device_id=(y, turn(z, d), x, c),
                device_id_type=MESH,
            )
            copy.start()
            sent.append(copy)
            slot = target.at[turn(z, -d)]
            small.append(
                pltpu.make_async_remote_copy(
                    src_ref=slot,
                    dst_ref=slot,
                    send_sem=send_s.at[index],
                    recv_sem=recv_s.at[index],
                    device_id=partner,
                    device_id_type=MESH,
                )
            )

    own["gain"].wait()
    own["obs_t"].wait()
    own["noise"].wait()
    put_split(gain_h, gain_l, ..., gain_v[...])
    rows_of = lax.broadcasted_iota(jnp.int32, (W, N), 0)
    cols_of = lax.broadcasted_iota(jnp.int32, (W, N), 1)
    start_row = x * 96 + c * W
    eye_rows = (rows_of + start_row == cols_of).astype(F32)
    cg[c, x] = eye_rows - product(obs_v[...], gain_h[...], gain_l[...], True)

    def fixed(part):
        rows = pl.ds(part * 128, 128)
        value = product(gain_v[rows, :] * on_v[...], gain_h[...], gain_l[...], True)
        put_split(fix_h, fix_l, rows, value)

    def send_gain(index, slot, device):
        copy = pltpu.make_async_remote_copy(
            src_ref=slot,
            dst_ref=slot,
            send_sem=send_c.at[index],
            recv_sem=recv_c.at[index],
            device_id=device,
            device_id_type=MESH,
        )
        copy.start()
        sent.append(copy)

    def recv_gain(index, slot):
        pltpu.make_async_remote_copy(
            src_ref=slot,
            dst_ref=slot,
            send_sem=send_c.at[index],
            recv_sem=recv_c.at[index],
            device_id=partner,
            device_id_type=MESH,
        ).wait_recv()

    for index, device in enumerate(x_to + [x_far, partner]):
        send_gain(index, cg.at[c, x], device)
    other.second(0, mixing.at[1])
    fixed(0)

    first.first_near()
    other.first_near()
    fixed(1)
    for index, d in enumerate((-1, 1, 2)):
        slot = cg.at[c, turn(x, d)]
        recv_gain(index, slot)
        send_gain(4 + index, slot, partner)
    first.second_near(0)
    other.second_near(0)
    fixed(2)
    first.first_far()
    other.first_far()

    for name in ("ret", "forc", "obs", "mn", "pm", "pf", "mix0", "mix1"):
        own[name].wait()
    for copy in small:
        copy.wait_recv()
    for place in range(4):
        for step in range(2):
            row = 2 * place + step
            ret8[pl.ds(row, 1), :] = ret4[place, pl.ds(step, 1), :]
            noise8[pl.ds(row, 1), :] = noise4[place, pl.ds(step, 1), :]
            forc16[pl.ds(row, 1), :] = forc4[place, pl.ds(step, 1), :]
            obs16[pl.ds(row, 1), :] = obs4[place, pl.ds(step, 1), :]

    recv_gain(3, cg.at[1 - c, x])
    for index, d in enumerate((-1, 1, 2)):
        recv_gain(4 + index, cg.at[1 - c, turn(x, d)])
    put_split(ct_h, ct_l, ..., jnp.concatenate([cg[core, place] for place in range(4) for core in range(2)], 0))
    offsets = product(forc16[...], ct_h[...], ct_l[...]) + product(obs16[...], gain_h[...], gain_l[...], True)
    off8[...] = offsets[:8]

    row_id = lax.broadcasted_iota(jnp.int32, (N, N), 0)
    col_id = lax.broadcasted_iota(jnp.int32, (N, N), 1)

    def step_first(ks):
        place = first.s[ks]
        raw = jnp.concatenate([ga[core, place, spot] for spot in range(4) for core in range(2)], 0)
        raw = raw + jnp.where(row_id == col_id, ret8[pl.ds(2 * place, 1), :], 0.0)
        put_split(b_h, b_l, 2 * place, product(raw, ct_h[...], ct_l[...]))

    def step_other(ks):
        place = other.s[ks]
        raw = jnp.concatenate(
            [
                gb[core, place, spot]
                + jnp.where(
                    rows_of + (place * 96 + core * W) == cols_of, ret8[pl.ds(2 * spot + 1, 1), :], 0.0
                )
                for spot in range(4)
                for core in range(2)
            ],
            0,
        )
        high, low = split(product(raw, ct_h[...], ct_l[...]))
        target = pl.ds(pl.multiple_of(place * 96, 32), 96)
        for spot in range(4):
            b_h[2 * spot + 1, target, :] = high[96 * spot : 96 * (spot + 1)]
            b_l[2 * spot + 1, target, :] = low[96 * spot : 96 * (spot + 1)]

    def ready(gather, ks):
        for kf in range(4):
            gather.shared(kf, ks)

    ready(first, 0)
    step_first(0)
    first.second_near(1)
    other.second_near(1)
    ready(other, 0)
    step_other(0)
    first.second_near(2)
    other.second_near(2)

    @pl.when(y == 0)
    def _():
        high, low = split(pf_v[...])
        put_split(p_h, p_l, ..., product(pf_v[...], high, low, True))

    first.second_near(3)
    other.second_near(3)
    ready(first, 1)
    step_first(1)
    first.second_far(0)
    other.second_far(0)
    ready(first, 2)
    step_first(2)
    first.second_far(1)
    other.second_far(1)
    ready(other, 1)
    step_other(1)
    first.second_far(2)
    other.second_far(2)
    ready(other, 2)
    step_other(2)
    first.second_far(3)
    other.second_far(3)
    ready(first, 3)
    step_first(3)
    ready(other, 3)
    step_other(3)

    row32 = lax.broadcasted_iota(jnp.int32, (32, N), 0)
    col32 = lax.broadcasted_iota(jnp.int32, (32, N), 1)
    start24 = (z * 4 + x) * CR
    walk = ((row32 < CR) & (row32 + start24 == col32)).astype(F32)
    for j in range(7, -1, -1):
        wc[j] = walk
        walk = product(walk, b_h[j], b_l[j], True)
    left = wc[...].reshape(256, N)
    spread = product(left, ct_h[...], ct_l[...], True).reshape(8, 32, N) * noise8[...].reshape(8, 1, N)
    noise = product(spread.reshape(256, N), ct_h[...], ct_l[...]) + product(left, fix_h[...], fix_l[...])
    gc[...] = noise.reshape(8, 32, N)

    @pl.when(y == 0)
    def _():
        begin = product(walk, p_h[...], p_l[...])
        stage[0] = jnp.where(row32 == CR, pm_v[...], begin)

    @pl.when(y != 0)
    def _():
        stage[0] = jnp.zeros((32, N), F32)

    grown = stage[0]
    for j in range(8):
        grown = product(grown, b_h[j], b_l[j])
        grown = grown + gc[j] + jnp.where(row32 == CR, off8[pl.ds(j, 1), :], 0.0)
    stage[1] = walk
    stage[2] = grown
    kind = 1 + c

    def ship(index, source, target, slot, device):
        return pltpu.make_async_remote_copy(
            src_ref=source,
            dst_ref=target,
            send_sem=send_y.at[index],
            recv_sem=recv_y.at[slot],
            device_id=device,
            device_id_type=MESH,
        )

    mine_a, mine_b = ea.at[c, z, x], eb.at[c, x, z]

    @pl.when(y == 0)
    def _():
        copies = []
        for d in range(3):
            copies.append(ship(3 * d, stage.at[2, pl.ds(8 - 8 * c + 0, 8)], mine_a.at[pl.ds(CR, 8)], 0, y_to[d]))
            copies.append(ship(3 * d + 1, stage.at[2, pl.ds(16, 8)], mine_b.at[pl.ds(CR, 8)], 1, y_to[d]))
            copies.append(ship(3 * d + 2, stage.at[2, pl.ds(CR, 8)], near_mean.at[0], 4, y_to[d]))
        for copy in copies:
            copy.start()
        for copy in copies:
            copy.wait_send()

    @pl.when(y == 1)
    def _():
        copies = []
        for d in range(2):
            copies.append(ship(2 * d, stage.at[kind, pl.ds(0, CR)], mine_a.at[pl.ds(0, CR)], 2, y_to[d]))
            copies.append(ship(2 * d + 1, stage.at[2, pl.ds(CR, 8)], near_mean.at[1], 5, y_to[d]))
        for copy in copies:
            copy.start()
        for copy in copies:
            copy.wait_send()

    @pl.when(y == 2)
    def _():
        copies = [
            ship(0, stage.at[kind, pl.ds(0, CR)], mine_b.at[pl.ds(0, CR)], 3, y_to[0]),
            ship(1, stage.at[2, pl.ds(CR, 8)], near_mean.at[2], 6, y_to[0]),
        ]
        for copy in copies:
            copy.start()
        for copy in copies:
            copy.wait_send()

    @pl.when(y >= 1)
    def _():
        ship(0, mine_a.at[pl.ds(CR, 8)], mine_a.at[pl.ds(CR, 8)], 0, partner).wait_recv()
        ship(0, mine_b.at[pl.ds(CR, 8)], mine_b.at[pl.ds(CR, 8)], 1, partner).wait_recv()
        ship(0, near_mean.at[0], near_mean.at[0], 4, partner).wait_recv()

    @pl.when(y >= 2)
    def _():
        ship(0, mine_a.at[pl.ds(0, CR)], mine_a.at[pl.ds(0, CR)], 2, partner).wait_recv()
        ship(0, near_mean.at[1], near_mean.at[1], 5, partner).wait_recv()

    @pl.when(y >= 3)
    def _():
        ship(0, mine_b.at[pl.ds(0, CR)], mine_b.at[pl.ds(0, CR)], 3, partner).wait_recv()
        ship(0, near_mean.at[2], near_mean.at[2], 6, partner).wait_recv()

    third = PlaneGather(lambda core, f, s: ea.at[core, s, f], 32, c, x, z, x_to, z_to, partner, send3, recv3, 0, sent)
    fourth = PlaneGather(
        lambda core, f, s: eb.at[core, s, f], 32, c, z, x, z_to, x_to, partner, send3, recv3, PER_CLASS, sent
    )
    for gather in (third, fourth):
        gather.first_own(gather.at(0, 0))
    for gather in (third, fourth):
        gather.second(0)
        gather.share(0, 0)

    last = 2 * z + 1
    wf[last, pl.ds(W, W), :] = eye_rows
    behind = product(eye_rows, b_h[last], b_l[last], True)
    w0_s[pl.ds(0, W), :] = eye_rows
    w0_s[pl.ds(W, W), :] = behind

    third.first_near()
    fourth.first_near()

    @pl.loop(0, 2 * z + 1)
    def _(i):
        j = 2 * z - i
        rows = w0_s[...]
        wf[j] = rows
        w0_s[...] = product(rows, b_h[j], b_l[j], True)

    third.second_near(0)
    fourth.second_near(0)
    third.first_far()
    fourth.first_far()

    def noise_rows(part):
        span = pl.ds(4 * part, 4)
        rows = wf[span].reshape(N, N)
        wide = product(rows, ct_h[...], ct_l[...], True).reshape(4, 96, N)
        wide = wide * noise8[pl.ds(4 * part, 4), :].reshape(4, 1, N)
        value = product(wide.reshape(N, N), ct_h[...], ct_l[...]) + product(rows, fix_h[...], fix_l[...])
        gf[span] = value.reshape(4, 96, N)

    noise_rows(0)
    for kf in (1, 2):
        third.second_near(kf)
        fourth.second_near(kf)

    @pl.when(z >= 2)
    def _():
        noise_rows(1)

    third.second_near(3)
    fourth.second_near(3)
    for kf in range(4):
        third.second_far(kf)
        fourth.second_far(kf)
    for ks in range(4):
        ready(third, ks)
        ready(fourth, ks)

    spots = [(a, b) for a in range(4) for b in range(4)]

    @pl.when(y == 3)
    def _():
        put_split(t2_h, t2_l, ..., jnp.concatenate([eb[0, b, a, pl.ds(0, CR), :] for a, b in spots], 0))
        put_split(n2_h, n2_l, ..., jnp.concatenate([eb[1, b, a, pl.ds(0, CR), :] for a, b in spots], 0))
        v2_s[...] = product(w0_s[...], t2_h[...], t2_l[...])

    @pl.when(y != 3)
    def _():
        v2_s[...] = w0_s[...]

    @pl.when(y >= 2)
    def _():
        put_split(t1_h, t1_l, ..., jnp.concatenate([ea[0, a, b, pl.ds(0, CR), :] for a, b in spots], 0))
        put_split(n1_h, n1_l, ..., jnp.concatenate([ea[1, a, b, pl.ds(0, CR), :] for a, b in spots], 0))
        v1_s[...] = product(v2_s[...], t1_h[...], t1_l[...])

    @pl.when(y < 2)
    def _():
        v1_s[...] = v2_s[...]

    @pl.when(y >= 1)
    def _():
        parts = []
        for a, b in spots:
            parts += [ea[1, a, b, pl.ds(CR, 8), :], ea[0, a, b, pl.ds(CR, 8), :], eb[0, b, a, pl.ds(CR, 8), :]]
        put_split(p_h, p_l, ..., jnp.concatenate(parts, 0))

    row16 = lax.broadcasted_iota(jnp.int32, (16, N), 0)

    def mean_rows(row):
        return jnp.where(row16 == 0, row, 0.0)

    xs[pl.ds(0, 96), :] = product(v1_s[...], p_h[...], p_l[...])

    @pl.when(y == 0)
    def _():
        xs[pl.ds(96, 16), :] = mean_rows(pm_v[...])

    @pl.when(y >= 1)
    def _():
        xs[pl.ds(96, 16), :] = mean_rows(near_mean[0, pl.ds(0, 1), :])

    @pl.when(y >= 2)
    def _():
        value = product(xs[...], t1_h[...], t1_l[...], True)
        added = product(v2_s[...], n1_h[...], n1_l[...])
        xs[...] = value + jnp.concatenate([added, mean_rows(near_mean[1, pl.ds(0, 1), :])], 0)

    @pl.when(y >= 3)
    def _():
        value = product(xs[...], t2_h[...], t2_l[...], True)
        added = product(w0_s[...], n2_h[...], n2_l[...])
        xs[...] = value + jnp.concatenate([added, mean_rows(near_mean[2, pl.ds(0, 1), :])], 0)

    @pl.loop(0, 2 * z + 1)
    def _(j):
        value = product(xs[...], b_h[j], b_l[j])
        xs[...] = value + jnp.concatenate([gf[j], mean_rows(off8[pl.ds(j, 1), :])], 0)

    covariances[0] = xs[pl.ds(0, W), :]
    means[pl.ds(0, 1), :] = xs[pl.ds(96, 1), :]
    value = product(xs[pl.ds(W, 64), :], b_h[last], b_l[last])
    covariances[1] = value[:W] + gf[last, pl.ds(W, W), :]
    means[pl.ds(1, 1), :] = value[W : W + 1] + off8[pl.ds(last, 1), :]

    for copy in sent:
        copy.wait_send()


def vmem(shape, dtype=F32):
    return pltpu.VMEM(shape, dtype)


def pair(shape):
    return [vmem(shape, BF16), vmem(shape, BF16)]


def per_device(mixing, retention, forcing, observations, model_noise, obs_noise, gain, obs_t, prior_mean, prior_factor):
    dma = pltpu.SemaphoreType.DMA
    square = (N, N)
    return pl.pallas_call(
        kernel,
        out_shape=(jax.ShapeDtypeStruct((2, N), F32), jax.ShapeDtypeStruct((2, W, N), F32)),
        in_specs=[pl.BlockSpec(memory_space=pl.ANY)] * 10,
        out_specs=(pl.BlockSpec(memory_space=pltpu.VMEM),) * 2,
        scratch_shapes=[
            vmem((2, 4, 4, W, N)),
            vmem((2, 4, 4, W, N)),
            vmem((2, 4, W, N)),
            vmem((2, 4, 4, 32, N)),
            vmem((2, 4, 4, 32, N)),
            vmem((4, 2, N)),
            vmem((4, 2, N)),
            vmem((4, 2, NOBS)),
            vmem((4, 2, N)),
            vmem((8, N)),
            vmem((16, N)),
            vmem((16, NOBS)),
            vmem((8, N)),
            vmem((1, NOBS)),
            vmem((N, NOBS)),
            *pair((N, NOBS)),
            vmem((W, NOBS)),
            vmem((1, N)),
            vmem(square),
            *pair(square),
            *pair(square),
            *pair(square),
            *pair((8, N, N)),
            vmem((8, N)),
            vmem((8, 32, N)),
            vmem((8, 32, N)),
            vmem((8, 96, N)),
            vmem((8, 96, N)),
            vmem((3, 32, N)),
            vmem((8, N)),
            vmem((3, 8, N)),
            *pair(square),
            *pair(square),
            *pair(square),
            *pair(square),
            vmem((96, N)),
            vmem((96, N)),
            vmem((96, N)),
            vmem((112, N)),
            dma((2 * PER_CLASS,)),
            dma((2 * PER_CLASS,)),
            dma((2 * PER_CLASS,)),
            dma((2 * PER_CLASS,)),
            dma((7,)),
            dma((7,)),
            dma((12,)),
            dma((12,)),
            dma((9,)),
            dma((7,)),
            dma((11,)),
        ],
        compiler_params=pltpu.CompilerParams(
            collective_id=0, has_side_effects=True, vmem_limit_bytes=67043328
        ),
        name="prefix",
    )(
        mixing, retention, forcing, observations, model_noise, obs_noise.reshape(1, NOBS), gain, obs_t,
        prior_mean.reshape(1, N), prior_factor,
    )


def solution(mesh):
    grid = Mesh(mesh.devices.reshape(4, 4, 4, 2), SEG + COL)
    placed = (
        P(SEG, COL, None),
        P(SEG, None),
        P(SEG, None),
        P(SEG, None),
        P(SEG, None),
        P(),
        P(),
        P(COL, None),
        P(),
        P(),
    )
    return jax.shard_map(
        per_device,
        mesh=grid,
        in_specs=placed,
        out_specs=(P(SEG, None), P(SEG, COL, None)),
        check_vma=False,
    )
```

```python
import functools

import jax
import jax.numpy as jnp
from jax import lax
from jax.experimental import pallas as pl
from jax.experimental.pallas import tpu as pltpu
from jax.sharding import Mesh
from jax.sharding import PartitionSpec as P

MESH = pl.DeviceIdType.MESH
F32 = jnp.float32
BF16 = jnp.bfloat16
SEG = ("y", "z")
COL = ("x", "c")
N = 384
NOBS = 1024
W = 48
CR = 24
PER_CLASS = 36
STRAIGHT1 = (3,)
STRAIGHT3 = (0, 1, 2, 3)


def split(value):
    high = value.astype(BF16)
    low = (value - high.astype(F32)).astype(BF16)
    return high, low


def dot(left, right, transposed):
    dims = (((1,), (1 if transposed else 0,)), ((), ()))
    return lax.dot_general(left, right, dims, preferred_element_type=F32)


def product(left, right_high, right_low, transposed=False):
    high, low = split(left)
    rows = left.shape[0]
    both = dot(jnp.concatenate([high, low], 0), right_high, transposed)
    return both[:rows] + (both[rows:] + dot(high, right_low, transposed))


def put_split(high_ref, low_ref, index, value):
    high, low = split(value)
    high_ref[index] = high
    low_ref[index] = low


def turn(position, by):
    return lax.rem(position + (by % 4), 4)


class PlaneGather:
    def __init__(self, unit, rows, core, first, second, to_first, to_second, partner, send, recv, base, sent, straight):
        self.unit, self.rows, self.core = unit, rows, core
        self.f = [turn(first, d) for d in (0, -1, 1, 2)]
        self.s = [turn(second, d) for d in (0, -1, 1, 2)]
        self.to_first, self.to_second, self.partner = to_first, to_second, partner
        self.send, self.recv, self.base, self.sent, self.straight = send, recv, base, sent, straight

    def at(self, kf, ks, half=None, core=None):
        ref = self.unit(self.core if core is None else core, self.f[kf], self.s[ks])
        if half is None:
            return ref
        middle = self.rows // 16 * 8
        return ref.at[pl.ds(0, middle)] if half == 0 else ref.at[pl.ds(middle, self.rows - middle)]

    def start(self, index, source, target, device):
        copy = pltpu.make_async_remote_copy(
            src_ref=source,
            dst_ref=target,
            send_sem=self.send.at[self.base + index],
            recv_sem=self.recv.at[self.base + index],
            device_id=device,
            device_id_type=MESH,
        )
        copy.start()
        self.sent.append(copy)

    def arrive(self, index, slot):
        pltpu.make_async_remote_copy(
            src_ref=slot,
            dst_ref=slot,
            send_sem=self.send.at[self.base + index],
            recv_sem=self.recv.at[self.base + index],
            device_id=self.partner,
            device_id_type=MESH,
        ).wait_recv()

    def first_own(self, source):
        for way in (0, 1):
            self.start(way, source, self.at(0, 0), self.to_first[way])

    def first_own_far(self, source):
        self.start(2, source, self.at(0, 0), self.to_first[2])

    def share(self, kf, ks, source=None):
        slot = self.at(kf, ks)
        self.start(20 + 4 * ks + kf, slot if source is None else source, slot, self.partner)

    def shared(self, kf, ks):
        self.arrive(20 + 4 * ks + kf, self.at(kf, ks, core=1 - self.core))

    def second(self, kf, source=None):
        slot = self.at(kf, 0)
        source = slot if source is None else source
        for way in (0, 1):
            self.start(4 + 2 * kf + way, source, slot, self.to_second[way])
        if kf in self.straight:
            self.start(12 + 2 * kf, source, slot, self.to_second[2])

    def first_near(self):
        for way in (0, 1):
            self.arrive(way, self.at(1 + way, 0))
            self.second(1 + way)
            self.share(1 + way, 0)

    def first_far(self):
        self.arrive(2, self.at(3, 0))
        self.second(3)
        self.share(3, 0)

    def second_near(self, kf):
        for way in (0, 1):
            self.arrive(4 + 2 * kf + way, self.at(kf, 1 + way))
            if kf not in self.straight:
                part = self.at(kf, 1 + way, half=way)
                self.start(12 + 2 * kf + way, part, part, self.to_second[way])
            self.share(kf, 1 + way)

    def second_far(self, kf):
        if kf in self.straight:
            self.arrive(12 + 2 * kf, self.at(kf, 3))
        else:
            for way in (0, 1):
                self.arrive(12 + 2 * kf + way, self.at(kf, 3, half=way))
        self.share(kf, 3)


def kernel(
    mixing, retention, forcing, observations, model_noise, obs_noise, gain, obs_t, prior_mean, prior_factor,
    out,
    ga, gb, cg, ea, eb, ret4, forc4, obs4, noise4, ret8, forc16, obs16, noise8, on_v, gain_v, gain_h, gain_l,
    obs_v, pm_v, pf_v, ct_h, ct_l, fix_h, fix_l, p_h, p_l, b_h, b_l, off8, wc, gc, wf, gf, stage,
    near_mean, t1_h, t1_l, n1_h, n1_l, t2_h, t2_l, n2_h, n2_l, w0_s, v1_s, v2_s, xs,
    send1, recv1, send3, recv3, send_c, recv_c, send_g, recv_g, send_s, recv_s, send_y, recv_y, send_m, recv_m, local,
):
    y, z, x, c = (lax.axis_index(name) for name in ("y", "z", "x", "c"))
    partner = (y, z, x, 1 - c)
    x_to = [(y, z, turn(x, d), c) for d in (1, -1, 2)]
    z_to = [(y, turn(z, d), x, c) for d in (1, -1, 2)]
    y_to = [(turn(y, d), z, x, c) for d in (1, 2, 3)]
    sent = []

    own = {}
    for index, (name, source, target) in enumerate(
        (
            ("gain", gain, gain_v),
            ("obs_t", obs_t, obs_v),
            ("mix0", mixing.at[0], ga.at[c, z, x]),
            ("mix1", mixing.at[1], gb.at[c, x, z]),
            ("noise", obs_noise, on_v),
            ("ret", retention, ret4.at[z]),
            ("forc", forcing, forc4.at[z]),
            ("obs", observations, obs4.at[z]),
            ("mn", model_noise, noise4.at[z]),
            ("pm", prior_mean, pm_v),
            ("pf", prior_factor, pf_v),
        )
    ):
        own[name] = pltpu.make_async_copy(source, target, local.at[index])
        own[name].start()

    ea[c, z, x] = jnp.zeros((CR, N), F32)
    eb[c, x, z] = jnp.zeros((CR, N), F32)
    forc16[...] = jnp.zeros((16, N), F32)
    obs16[...] = jnp.zeros((16, NOBS), F32)

    barrier = pltpu.get_barrier_semaphore()
    friends = [partner] + x_to + z_to + y_to
    for friend in friends:
        pl.semaphore_signal(barrier, inc=1, device_id=friend, device_id_type=MESH)

    own["gain"].wait()
    own["obs_t"].wait()
    own["noise"].wait()
    put_split(gain_h, gain_l, ..., gain_v[...])
    rows_of = lax.broadcasted_iota(jnp.int32, (W, N), 0)
    cols_of = lax.broadcasted_iota(jnp.int32, (W, N), 1)
    start_row = x * 96 + c * W
    eye_rows = (rows_of + start_row == cols_of).astype(F32)
    cg[c, x] = eye_rows - product(obs_v[...], gain_h[...], gain_l[...], True)
    for part in range(3):
        rows = pl.ds(part * 128, 128)
        put_split(fix_h, fix_l, rows, product(gain_v[rows, :] * on_v[...], gain_h[...], gain_l[...], True))

    own["pf"].wait()

    @pl.when(y == 0)
    def _():
        high, low = split(pf_v[...])
        put_split(p_h, p_l, ..., product(pf_v[...], high, low, True))

    pl.semaphore_wait(barrier, len(friends))

    first = PlaneGather(lambda core, f, s: ga.at[core, s, f], W, c, x, z, x_to, z_to, partner, send1, recv1, 0, sent, STRAIGHT1)
    other = PlaneGather(
        lambda core, f, s: gb.at[core, s, f], W, c, z, x, z_to, x_to, partner, send1, recv1, PER_CLASS, sent, STRAIGHT1
    )

    def gain_copy(index, slot, device):
        return pltpu.make_async_remote_copy(
            src_ref=slot,
            dst_ref=slot,
            send_sem=send_c.at[index],
            recv_sem=recv_c.at[index],
            device_id=device,
            device_id_type=MESH,
        )

    def third_of(place, part):
        return cg.at[c, place, pl.ds(16 * part, 16)]

    @pl.when(y < 3)
    def _():
        for index, device in enumerate(x_to):
            gain_copy(index, third_of(x, y), device).start()

    for gather, step in ((first, 0), (other, 1)):
        gather.first_own(mixing.at[step])
    for gather, step in ((first, 0), (other, 1)):
        gather.first_own_far(mixing.at[step])
    for gather, step in ((first, 0), (other, 1)):
        gather.second(0, mixing.at[step])
    gain_copy(3, cg.at[c, x], partner).start()
    for gather, step in ((first, 0), (other, 1)):
        gather.share(0, 0, mixing.at[step])

    small = []
    for array, (source, target) in enumerate(
        ((retention, ret4), (forcing, forc4), (observations, obs4), (model_noise, noise4))
    ):
        for d in (1, 2, 3):
            index = 3 * array + d - 1
            copy = pltpu.make_async_remote_copy(
                src_ref=source,
                dst_ref=target.at[z],
                send_sem=send_s.at[index],
                recv_sem=recv_s.at[index],
                device_id=(y, turn(z, d), x, c),
                device_id_type=MESH,
            )
            copy.start()
            sent.append(copy)
            slot = target.at[turn(z, -d)]
            small.append(
                pltpu.make_async_remote_copy(
                    src_ref=slot,
                    dst_ref=slot,
                    send_sem=send_s.at[index],
                    recv_sem=recv_s.at[index],
                    device_id=partner,
                    device_id_type=MESH,
                )
            )


    @pl.when(y < 3)
    def _():
        for index, d in enumerate((-1, 1, 2)):
            slot = third_of(turn(x, d), y)
            gain_copy(index, slot, partner).wait_recv()
            for way in range(3):
                copy = pltpu.make_async_remote_copy(
                    src_ref=slot,
                    dst_ref=slot,
                    send_sem=send_g.at[3 * way + index],
                    recv_sem=recv_g.at[3 * y + index],
                    device_id=y_to[way],
                    device_id_type=MESH,
                )
                copy.start()

    def drain():
        for copy in sent:
            copy.wait_send()

        @pl.when(c == 0)
        def _():
            ships(True, lambda copy: copy.wait_send())

        @pl.when(c == 1)
        def _():
            ships(False, lambda copy: copy.wait_send())
            for plane in range(3):

                @pl.when(y > plane)
                def _():
                    pass_mean(plane).wait_send()

        @pl.when(y < 3)
        def _():
            for index, device in enumerate(x_to):
                gain_copy(index, third_of(x, y), device).wait_send()
            for index, d in enumerate((-1, 1, 2)):
                slot = third_of(turn(x, d), y)
                for way in range(3):
                    pltpu.make_async_remote_copy(
                        src_ref=slot,
                        dst_ref=slot,
                        send_sem=send_g.at[3 * way + index],
                        recv_sem=recv_g.at[3 * y + index],
                        device_id=y_to[way],
                        device_id_type=MESH,
                    ).wait_send()

        for index in range(3):
            gain_copy(4 + index, cg.at[c, x], partner).wait_send()
        gain_copy(3, cg.at[c, x], partner).wait_send()

    first.first_near()
    other.first_near()
    first.first_far()
    other.first_far()
    first.second_near(0)
    other.second_near(0)
    for part in range(3):

        @pl.when(y != part)
        def _():
            for index, d in enumerate((-1, 1, 2)):
                slot = third_of(turn(x, d), part)
                pltpu.make_async_remote_copy(
                    src_ref=slot,
                    dst_ref=slot,
                    send_sem=send_g.at[0],
                    recv_sem=recv_g.at[3 * part + index],
                    device_id=partner,
                    device_id_type=MESH,
                ).wait_recv()

    for index, d in enumerate((-1, 1, 2)):
        gain_copy(4 + index, cg.at[c, turn(x, d)], partner).start()

    for name in ("ret", "forc", "obs", "mn", "pm", "mix0", "mix1"):
        own[name].wait()
    for copy in small:
        copy.wait_recv()
    for place in range(4):
        for step in range(2):
            row = 2 * place + step
            ret8[pl.ds(row, 1), :] = ret4[place, pl.ds(step, 1), :]
            noise8[pl.ds(row, 1), :] = noise4[place, pl.ds(step, 1), :]
            forc16[pl.ds(row, 1), :] = forc4[place, pl.ds(step, 1), :]
            obs16[pl.ds(row, 1), :] = obs4[place, pl.ds(step, 1), :]

    gain_copy(3, cg.at[1 - c, x], partner).wait_recv()
    for index, d in enumerate((-1, 1, 2)):
        gain_copy(4 + index, cg.at[1 - c, turn(x, d)], partner).wait_recv()
    put_split(ct_h, ct_l, ..., jnp.concatenate([cg[core, place] for place in range(4) for core in range(2)], 0))
    offsets = product(forc16[...], ct_h[...], ct_l[...]) + product(obs16[...], gain_h[...], gain_l[...], True)
    off8[...] = offsets[:8]

    row_id = lax.broadcasted_iota(jnp.int32, (N, N), 0)
    col_id = lax.broadcasted_iota(jnp.int32, (N, N), 1)

    def step_first(ks):
        place = first.s[ks]
        raw = jnp.concatenate([ga[core, place, spot] for spot in range(4) for core in range(2)], 0)
        raw = raw + jnp.where(row_id == col_id, ret8[pl.ds(2 * place, 1), :], 0.0)
        put_split(b_h, b_l, 2 * place, product(raw, ct_h[...], ct_l[...]))

    def step_other(ks):
        place = other.s[ks]
        raw = jnp.concatenate(
            [
                gb[core, place, spot]
                + jnp.where(
                    rows_of + (place * 96 + core * W) == cols_of, ret8[pl.ds(2 * spot + 1, 1), :], 0.0
                )
                for spot in range(4)
                for core in range(2)
            ],
            0,
        )
        high, low = split(product(raw, ct_h[...], ct_l[...]))
        target = pl.ds(pl.multiple_of(place * 96, 32), 96)
        for spot in range(4):
            b_h[2 * spot + 1, target, :] = high[96 * spot : 96 * (spot + 1)]
            b_l[2 * spot + 1, target, :] = low[96 * spot : 96 * (spot + 1)]

    def ready(gather, ks):
        for kf in range(4):
            gather.shared(kf, ks)

    ready(first, 0)
    step_first(0)
    first.second_near(1)
    other.second_near(1)
    ready(other, 0)
    step_other(0)
    first.second_near(2)
    other.second_near(2)

    first.second_near(3)
    other.second_near(3)
    ready(first, 1)
    step_first(1)
    first.second_far(0)
    other.second_far(0)
    ready(first, 2)
    step_first(2)
    first.second_far(1)
    other.second_far(1)
    ready(other, 1)
    step_other(1)
    first.second_far(2)
    other.second_far(2)
    ready(other, 2)
    step_other(2)
    first.second_far(3)
    other.second_far(3)
    ready(first, 3)
    step_first(3)
    ready(other, 3)
    step_other(3)

    row32 = lax.broadcasted_iota(jnp.int32, (32, N), 0)
    col32 = lax.broadcasted_iota(jnp.int32, (32, N), 1)
    start24 = (z * 4 + x) * CR
    walk = ((row32 < CR) & (row32 + start24 == col32)).astype(F32)
    for j in range(7, -1, -1):
        wc[j] = walk
        walk = product(walk, b_h[j], b_l[j], True)
    stage[1] = walk
    mine_a, mine_b = ea.at[c, z, x], eb.at[c, x, z]

    def ship(index, source, target, slot, device):
        return pltpu.make_async_remote_copy(
            src_ref=source,
            dst_ref=target,
            send_sem=send_y.at[index],
            recv_sem=recv_y.at[slot],
            device_id=device,
            device_id_type=MESH,
        )

    def ships(first_core, act):
        near, far = pl.ds(0, 256), pl.ds(256, 128)
        if first_core:

            @pl.when(y == 1)
            def _():
                for d in range(2):
                    act(ship(d, stage.at[1, pl.ds(0, CR)], mine_a, 2, y_to[d]))

            @pl.when(y == 2)
            def _():
                act(ship(0, stage.at[1, pl.ds(0, CR)], mine_b, 3, y_to[0]))

            return
        packed, mean = stage.at[2, pl.ds(0, CR)], stage.at[0, pl.ds(CR, 8)]

        @pl.when(y == 0)
        def _():
            for d in range(3):
                act(ship(3 * d, packed.at[:, pl.ds(0, 128)], mine_a.at[:, far], 0, y_to[d]))
                act(ship(3 * d + 1, packed.at[:, pl.ds(128, 128)], mine_b.at[:, far], 1, y_to[d]))
                act(ship(3 * d + 2, mean, near_mean.at[0], 4, y_to[d]))

        @pl.when(y == 1)
        def _():
            for d in range(2):
                act(ship(2 * d, packed.at[:, near], mine_a.at[:, near], 2, y_to[d]))
                act(ship(2 * d + 1, mean, near_mean.at[1], 5, y_to[d]))

        @pl.when(y == 2)
        def _():
            act(ship(0, packed.at[:, near], mine_b.at[:, near], 3, y_to[0]))
            act(ship(1, mean, near_mean.at[2], 6, y_to[0]))

    def pass_mean(index):
        return pltpu.make_async_remote_copy(
            src_ref=near_mean.at[index],
            dst_ref=near_mean.at[index],
            send_sem=send_m.at[index],
            recv_sem=recv_m.at[index],
            device_id=partner,
            device_id_type=MESH,
        )

    @pl.when(c == 0)
    def _():
        ships(True, lambda copy: copy.start())

    @pl.when(c == 1)
    def _():
        left = wc[...].reshape(256, N)
        spread = product(left, ct_h[...], ct_l[...], True).reshape(8, 32, N) * noise8[...].reshape(8, 1, N)
        noise = product(spread.reshape(256, N), ct_h[...], ct_l[...]) + product(left, fix_h[...], fix_l[...])
        gc[...] = noise.reshape(8, 32, N)

        @pl.when(y == 0)
        def _():
            begin = product(stage[1], p_h[...], p_l[...])
            stage[0] = jnp.where(row32 == CR, pm_v[...].reshape(1, N), begin)

        @pl.when(y != 0)
        def _():
            stage[0] = jnp.zeros((32, N), F32)

        grown = stage[0]
        for j in range(8):
            grown = product(grown, b_h[j], b_l[j])
            grown = grown + gc[j] + jnp.where(row32 == CR, off8[pl.ds(j, 1), :], 0.0)
        stage[0] = grown
        band = row32[:, :128] + start24
        low, high = band < 128, band >= 256
        one, two, three = (grown[:, 128 * b : 128 * (b + 1)] for b in range(3))
        stage[2, :, pl.ds(0, 128)] = jnp.where(low, one, jnp.where(high, three, two))
        stage[2, :, pl.ds(128, 128)] = jnp.where(low, two, jnp.where(high, one, three))
        ships(False, lambda copy: copy.start())

    @pl.when((c == 0) & (y >= 2))
    def _():
        ship(0, mine_a, mine_a, 2, partner).wait_recv()

    @pl.when((c == 0) & (y >= 3))
    def _():
        ship(0, mine_b, mine_b, 3, partner).wait_recv()

    @pl.when((c == 1) & (y >= 1))
    def _():
        ship(0, mine_a.at[:, pl.ds(256, 128)], mine_a.at[:, pl.ds(256, 128)], 0, partner).wait_recv()
        ship(0, mine_b.at[:, pl.ds(256, 128)], mine_b.at[:, pl.ds(256, 128)], 1, partner).wait_recv()

    @pl.when((c == 1) & (y >= 2))
    def _():
        ship(0, mine_a.at[:, pl.ds(0, 256)], mine_a.at[:, pl.ds(0, 256)], 2, partner).wait_recv()

    @pl.when((c == 1) & (y >= 3))
    def _():
        ship(0, mine_b.at[:, pl.ds(0, 256)], mine_b.at[:, pl.ds(0, 256)], 3, partner).wait_recv()

    third = PlaneGather(lambda core, f, s: ea.at[core, s, f], CR, c, x, z, x_to, z_to, partner, send3, recv3, 0, sent, STRAIGHT3)
    fourth = PlaneGather(
        lambda core, f, s: eb.at[core, s, f], CR, c, z, x, z_to, x_to, partner, send3, recv3, PER_CLASS, sent, STRAIGHT3
    )
    for gather in (third, fourth):
        gather.first_own(gather.at(0, 0))
    for gather in (third, fourth):
        gather.first_own_far(gather.at(0, 0))
    for gather in (third, fourth):
        gather.second(0)
        gather.share(0, 0)

    for plane in range(3):

        @pl.when((c == 1) & (y > plane))
        def _():
            ship(0, near_mean.at[plane], near_mean.at[plane], 4 + plane, partner).wait_recv()
            pass_mean(plane).start()

    last = 2 * z + 1
    wf[last, pl.ds(W, W), :] = eye_rows
    behind = product(eye_rows, b_h[last], b_l[last], True)
    w0_s[pl.ds(0, W), :] = eye_rows
    w0_s[pl.ds(W, W), :] = behind

    third.first_near()
    fourth.first_near()
    third.first_far()
    fourth.first_far()

    @pl.loop(0, 2 * z + 1)
    def _(i):
        j = 2 * z - i
        rows = w0_s[...]
        wf[j] = rows
        w0_s[...] = product(rows, b_h[j], b_l[j], True)

    def noise_rows(part):
        span = pl.ds(4 * part, 4)
        rows = wf[span].reshape(N, N)
        wide = product(rows, ct_h[...], ct_l[...], True).reshape(4, 96, N)
        wide = wide * noise8[pl.ds(4 * part, 4), :].reshape(4, 1, N)
        value = product(wide.reshape(N, N), ct_h[...], ct_l[...]) + product(rows, fix_h[...], fix_l[...])
        gf[span] = value.reshape(4, 96, N)

    third.second_near(0)
    fourth.second_near(0)
    noise_rows(0)
    for kf in (1, 2):
        third.second_near(kf)
        fourth.second_near(kf)

    @pl.when(z >= 2)
    def _():
        noise_rows(1)

    third.second_near(3)
    fourth.second_near(3)
    for kf in range(4):
        third.second_far(kf)
        fourth.second_far(kf)
    for ks in range(4):
        ready(third, ks)
        ready(fourth, ks)

    spots = [(a, b) for a in range(4) for b in range(4)]

    for plane in range(3):

        @pl.when((c == 0) & (y > plane))
        def _():
            pass_mean(plane).wait_recv()

    def symmetric(own, after):
        d0, d1, d2 = (own[128 * b : 128 * (b + 1)] for b in range(3))
        u0, u1, u2 = (after[128 * b : 128 * (b + 1)] for b in range(3))
        rows = ((d0, u0, u2.T), (u0.T, d1, u1), (u2, u1.T, d2))
        return jnp.concatenate([jnp.concatenate(row, 1) for row in rows], 0)

    def columns(pick, block):
        return jnp.concatenate([pick(a, b)[:, 128 * block : 128 * (block + 1)] for a, b in spots], 0)

    def from_a(a, b):
        return ea[1, a, b]

    def from_b(a, b):
        return eb[1, b, a]

    @pl.when(y == 3)
    def _():
        put_split(t2_h, t2_l, ..., jnp.concatenate([eb[0, b, a] for a, b in spots], 0))
        put_split(n2_h, n2_l, ..., symmetric(columns(from_b, 0), columns(from_b, 1)))
        v2_s[...] = product(w0_s[...], t2_h[...], t2_l[...])

    @pl.when(y != 3)
    def _():
        v2_s[...] = w0_s[...]

    @pl.when(y >= 2)
    def _():
        put_split(t1_h, t1_l, ..., jnp.concatenate([ea[0, a, b] for a, b in spots], 0))
        put_split(n1_h, n1_l, ..., symmetric(columns(from_a, 0), columns(from_a, 1)))
        v1_s[...] = product(v2_s[...], t1_h[...], t1_l[...])

    @pl.when(y < 2)
    def _():
        v1_s[...] = v2_s[...]

    @pl.when(y >= 1)
    def _():
        put_split(p_h, p_l, ..., symmetric(columns(from_a, 2), columns(from_b, 2)))

    row16 = lax.broadcasted_iota(jnp.int32, (16, N), 0)

    def mean_rows(row):
        return jnp.where(row16 == 0, row, 0.0)

    xs[pl.ds(0, 96), :] = product(v1_s[...], p_h[...], p_l[...])

    @pl.when(y == 0)
    def _():
        xs[pl.ds(96, 16), :] = mean_rows(pm_v[...].reshape(1, N))

    @pl.when(y >= 1)
    def _():
        xs[pl.ds(96, 16), :] = mean_rows(near_mean[0, pl.ds(0, 1), :])

    @pl.when(y >= 2)
    def _():
        value = product(xs[...], t1_h[...], t1_l[...], True)
        added = product(v2_s[...], n1_h[...], n1_l[...])
        xs[...] = value + jnp.concatenate([added, mean_rows(near_mean[1, pl.ds(0, 1), :])], 0)

    @pl.when(y >= 3)
    def _():
        value = product(xs[...], t2_h[...], t2_l[...], True)
        added = product(w0_s[...], n2_h[...], n2_l[...])
        xs[...] = value + jnp.concatenate([added, mean_rows(near_mean[2, pl.ds(0, 1), :])], 0)

    @pl.loop(0, 2 * z + 1)
    def _(j):
        value = product(xs[...], b_h[j], b_l[j])
        xs[...] = value + jnp.concatenate([gf[j], mean_rows(off8[pl.ds(j, 1), :])], 0)

    out[pl.ds(0, W), :] = xs[pl.ds(0, W), :]
    out[pl.ds(96, 1), :] = xs[pl.ds(96, 1), :]
    value = product(xs[pl.ds(W, 64), :], b_h[last], b_l[last])
    out[pl.ds(W, W), :] = value[:W] + gf[last, pl.ds(W, W), :]
    out[pl.ds(97, 1), :] = value[W : W + 1] + off8[pl.ds(last, 1), :]
    drain()


def finish(rows, means, covariances):
    covariances[0] = rows[pl.ds(0, W), :]
    covariances[1] = rows[pl.ds(W, W), :]
    means[...] = rows[pl.ds(96, 2), :]


def vmem(shape, dtype=F32):
    return pltpu.VMEM(shape, dtype)


def pair(shape):
    return [vmem(shape, BF16), vmem(shape, BF16)]


def per_device(mixing, retention, forcing, observations, model_noise, obs_noise, gain, obs_t, prior_mean, prior_factor):
    dma = pltpu.SemaphoreType.DMA
    square = (N, N)
    rows = pl.pallas_call(
        kernel,
        out_shape=jax.ShapeDtypeStruct((104, N), F32),
        in_specs=[pl.BlockSpec(memory_space=pl.ANY)] * 10,
        out_specs=pl.BlockSpec(memory_space=pltpu.VMEM),
        scratch_shapes=[
            vmem((2, 4, 4, W, N)),
            vmem((2, 4, 4, W, N)),
            vmem((2, 4, W, N)),
            vmem((2, 4, 4, CR, N)),
            vmem((2, 4, 4, CR, N)),
            vmem((4, 2, N)),
            vmem((4, 2, N)),
            vmem((4, 2, NOBS)),
            vmem((4, 2, N)),
            vmem((8, N)),
            vmem((16, N)),
            vmem((16, NOBS)),
            vmem((8, N)),
            vmem((1, NOBS)),
            vmem((N, NOBS)),
            *pair((N, NOBS)),
            vmem((W, NOBS)),
            vmem((N,)),
            vmem(square),
            *pair(square),
            *pair(square),
            *pair(square),
            *pair((8, N, N)),
            vmem((8, N)),
            vmem((8, 32, N)),
            vmem((8, 32, N)),
            vmem((8, 96, N)),
            vmem((8, 96, N)),
            vmem((3, 32, N)),
            vmem((3, 8, N)),
            *pair(square),
            *pair(square),
            *pair(square),
            *pair(square),
            vmem((96, N)),
            vmem((96, N)),
            vmem((96, N)),
            vmem((112, N)),
            dma((2 * PER_CLASS,)),
            dma((2 * PER_CLASS,)),
            dma((2 * PER_CLASS,)),
            dma((2 * PER_CLASS,)),
            dma((7,)),
            dma((7,)),
            dma((9,)),
            dma((9,)),
            dma((12,)),
            dma((12,)),
            dma((9,)),
            dma((7,)),
            dma((3,)),
            dma((3,)),
            dma((11,)),
        ],
        compiler_params=pltpu.CompilerParams(
            collective_id=0, has_side_effects=True, vmem_limit_bytes=67043328
        ),
        name="prefix",
    )(
        mixing, retention, forcing, observations, model_noise, obs_noise.reshape(1, NOBS), gain, obs_t,
        prior_mean, prior_factor,
    )
    return pl.pallas_call(
        finish,
        out_shape=(jax.ShapeDtypeStruct((2, N), F32), jax.ShapeDtypeStruct((2, W, N), F32)),
        in_specs=[pl.BlockSpec(memory_space=pltpu.VMEM)],
        out_specs=(pl.BlockSpec(memory_space=pltpu.VMEM),) * 2,
        name="finish",
    )(rows)


def solution(mesh):
    grid = Mesh(mesh.devices.reshape(4, 4, 4, 2), SEG + COL)
    placed = (
        P(SEG, COL, None),
        P(SEG, None),
        P(SEG, None),
        P(SEG, None),
        P(SEG, None),
        P(),
        P(),
        P(COL, None),
        P(),
        P(),
    )
    return jax.shard_map(
        per_device,
        mesh=grid,
        in_specs=placed,
        out_specs=(P(SEG, None), P(SEG, COL, None)),
        check_vma=False,
    )
```

```python
import functools

import jax
import jax.numpy as jnp
from jax import lax
from jax.experimental import pallas as pl
from jax.experimental.pallas import tpu as pltpu
from jax.sharding import Mesh
from jax.sharding import PartitionSpec as P

MESH = pl.DeviceIdType.MESH
F32 = jnp.float32
BF16 = jnp.bfloat16
SEG = ("y", "z")
COL = ("x", "c")
N = 384
NOBS = 1024
W = 48
CR = 24
PER_CLASS = 36
STRAIGHT1 = (3,)
STRAIGHT3 = (0, 1, 2, 3)


def split(value):
    high = value.astype(BF16)
    low = (value - high.astype(F32)).astype(BF16)
    return high, low


def dot(left, right, transposed):
    dims = (((1,), (1 if transposed else 0,)), ((), ()))
    return lax.dot_general(left, right, dims, preferred_element_type=F32)


def product(left, right_high, right_low, transposed=False):
    high, low = split(left)
    rows = left.shape[0]
    both = dot(jnp.concatenate([high, low], 0), right_high, transposed)
    return both[:rows] + (both[rows:] + dot(high, right_low, transposed))


def put_split(high_ref, low_ref, index, value):
    high, low = split(value)
    high_ref[index] = high
    low_ref[index] = low


def turn(position, by):
    return lax.rem(position + (by % 4), 4)


class PlaneGather:
    def __init__(self, unit, rows, core, first, second, to_first, to_second, partner, send, recv, base, sent, straight, sharing=True):
        self.unit, self.rows, self.core = unit, rows, core
        self.f = [turn(first, d) for d in (0, -1, 1, 2)]
        self.s = [turn(second, d) for d in (0, -1, 1, 2)]
        self.to_first, self.to_second, self.partner = to_first, to_second, partner
        self.send, self.recv, self.base, self.sent, self.straight = send, recv, base, sent, straight
        self.sharing = sharing

    def at(self, kf, ks, half=None, core=None):
        ref = self.unit(self.core if core is None else core, self.f[kf], self.s[ks])
        if half is None:
            return ref
        middle = self.rows // 16 * 8
        return ref.at[pl.ds(0, middle)] if half == 0 else ref.at[pl.ds(middle, self.rows - middle)]

    def start(self, index, source, target, device):
        copy = pltpu.make_async_remote_copy(
            src_ref=source,
            dst_ref=target,
            send_sem=self.send.at[self.base + index],
            recv_sem=self.recv.at[self.base + index],
            device_id=device,
            device_id_type=MESH,
        )
        copy.start()
        self.sent.append(copy)

    def arrive(self, index, slot):
        pltpu.make_async_remote_copy(
            src_ref=slot,
            dst_ref=slot,
            send_sem=self.send.at[self.base + index],
            recv_sem=self.recv.at[self.base + index],
            device_id=self.partner,
            device_id_type=MESH,
        ).wait_recv()

    def first_own(self, source):
        for way in (0, 1):
            self.start(way, source, self.at(0, 0), self.to_first[way])

    def first_own_far(self, source):
        self.start(2, source, self.at(0, 0), self.to_first[2])

    def share(self, kf, ks, source=None):
        if not self.sharing:
            return
        slot = self.at(kf, ks)
        self.start(20 + 4 * ks + kf, slot if source is None else source, slot, self.partner)

    def shared(self, kf, ks):
        self.arrive(20 + 4 * ks + kf, self.at(kf, ks, core=1 - self.core))

    def second(self, kf, source=None):
        slot = self.at(kf, 0)
        source = slot if source is None else source
        for way in (0, 1):
            self.start(4 + 2 * kf + way, source, slot, self.to_second[way])
        if kf in self.straight:
            self.start(12 + 2 * kf, source, slot, self.to_second[2])

    def first_near(self):
        for way in (0, 1):
            self.arrive(way, self.at(1 + way, 0))
            self.second(1 + way)
            self.share(1 + way, 0)

    def first_far(self):
        self.arrive(2, self.at(3, 0))
        self.second(3)
        self.share(3, 0)

    def second_near(self, kf):
        for way in (0, 1):
            self.arrive(4 + 2 * kf + way, self.at(kf, 1 + way))
            if kf not in self.straight:
                part = self.at(kf, 1 + way, half=way)
                self.start(12 + 2 * kf + way, part, part, self.to_second[way])
            self.share(kf, 1 + way)

    def second_far(self, kf):
        if kf in self.straight:
            self.arrive(12 + 2 * kf, self.at(kf, 3))
        else:
            for way in (0, 1):
                self.arrive(12 + 2 * kf + way, self.at(kf, 3, half=way))
        self.share(kf, 3)


def kernel(
    mixing, retention, forcing, observations, model_noise, obs_noise, gain, obs_t, prior_mean, prior_factor,
    means, covariances,
    ga, gb, gx, cg, ea, eb, ret4, forc4, obs4, noise4, ret8, forc16, obs16, noise8, on_v, gain_v, gain_h, gain_l,
    obs_v, pm_v, pf_v, ct_h, ct_l, fix_h, fix_l, p_h, p_l, b_h, b_l, off8, wc, gc, wf, gf, stage,
    near_mean, t1_h, t1_l, n1_h, n1_l, t2_h, t2_l, n2_h, n2_l, w0_s, v1_s, v2_s, xs,
    send1, recv1, send3, recv3, send_c, recv_c, send_g, recv_g, send_s, recv_s, send_y, recv_y, send_m, recv_m, send_b, recv_b, local,
):
    y, z, x, c = (lax.axis_index(name) for name in ("y", "z", "x", "c"))
    partner = (y, z, x, 1 - c)
    x_to = [(y, z, turn(x, d), c) for d in (1, -1, 2)]
    z_to = [(y, turn(z, d), x, c) for d in (1, -1, 2)]
    y_to = [(turn(y, d), z, x, c) for d in (1, 2, 3)]
    sent = []

    own = {}
    for index, (name, source, target) in enumerate(
        (
            ("gain", gain, gain_v),
            ("obs_t", obs_t, obs_v),
            ("mix0", mixing.at[0], ga.at[c, z, x]),
            ("mix1", mixing.at[1], gb.at[c, x, z]),
            ("noise", obs_noise, on_v),
            ("ret", retention, ret4.at[z]),
            ("forc", forcing, forc4.at[z]),
            ("obs", observations, obs4.at[z]),
            ("mn", model_noise, noise4.at[z]),
            ("pm", prior_mean, pm_v),
            ("pf", prior_factor, pf_v),
        )
    ):
        own[name] = pltpu.make_async_copy(source, target, local.at[index])
        own[name].start()

    ea[c, z, x] = jnp.zeros((CR, N), F32)
    eb[c, x, z] = jnp.zeros((CR, N), F32)
    forc16[...] = jnp.zeros((16, N), F32)
    obs16[...] = jnp.zeros((16, NOBS), F32)

    barrier = pltpu.get_barrier_semaphore()
    friends = [partner] + x_to + z_to + y_to
    for friend in friends:
        pl.semaphore_signal(barrier, inc=1, device_id=friend, device_id_type=MESH)

    own["gain"].wait()
    own["obs_t"].wait()
    own["noise"].wait()
    put_split(gain_h, gain_l, ..., gain_v[...])
    rows_of = lax.broadcasted_iota(jnp.int32, (W, N), 0)
    cols_of = lax.broadcasted_iota(jnp.int32, (W, N), 1)
    start_row = x * 96 + c * W
    eye_rows = (rows_of + start_row == cols_of).astype(F32)
    cg[c, x] = eye_rows - product(obs_v[...], gain_h[...], gain_l[...], True)
    for part in range(3):
        rows = pl.ds(part * 128, 128)
        put_split(fix_h, fix_l, rows, product(gain_v[rows, :] * on_v[...], gain_h[...], gain_l[...], True))

    own["pf"].wait()

    @pl.when(y == 0)
    def _():
        high, low = split(pf_v[...])
        put_split(p_h, p_l, ..., product(pf_v[...], high, low, True))

    pl.semaphore_wait(barrier, len(friends))

    first = PlaneGather(lambda core, f, s: ga.at[core, s, f], W, c, x, z, x_to, z_to, partner, send1, recv1, 0, sent, STRAIGHT1, False)
    other = PlaneGather(
        lambda core, f, s: gb.at[core, s, f], W, c, z, x, z_to, x_to, partner, send1, recv1, PER_CLASS, sent, STRAIGHT1, False
    )

    def gain_copy(index, slot, device):
        return pltpu.make_async_remote_copy(
            src_ref=slot,
            dst_ref=slot,
            send_sem=send_c.at[index],
            recv_sem=recv_c.at[index],
            device_id=device,
            device_id_type=MESH,
        )

    def third_of(place, part):
        return cg.at[c, place, pl.ds(16 * part, 16)]

    @pl.when(y < 3)
    def _():
        for index, device in enumerate(x_to):
            gain_copy(index, third_of(x, y), device).start()

    for gather, step in ((first, 0), (other, 1)):
        gather.first_own(mixing.at[step])
    for gather, step in ((first, 0), (other, 1)):
        gather.first_own_far(mixing.at[step])
    for gather, step in ((first, 0), (other, 1)):
        gather.second(0, mixing.at[step])
    gain_copy(3, cg.at[c, x], partner).start()
    for gather, step in ((first, 0), (other, 1)):
        gather.share(0, 0, mixing.at[step])

    small = []
    for array, (source, target) in enumerate(
        ((retention, ret4), (forcing, forc4), (observations, obs4), (model_noise, noise4))
    ):
        for d in (1, 2, 3):
            index = 3 * array + d - 1
            copy = pltpu.make_async_remote_copy(
                src_ref=source,
                dst_ref=target.at[z],
                send_sem=send_s.at[index],
                recv_sem=recv_s.at[index],
                device_id=(y, turn(z, d), x, c),
                device_id_type=MESH,
            )
            copy.start()
            sent.append(copy)
            slot = target.at[turn(z, -d)]
            small.append(
                pltpu.make_async_remote_copy(
                    src_ref=slot,
                    dst_ref=slot,
                    send_sem=send_s.at[index],
                    recv_sem=recv_s.at[index],
                    device_id=partner,
                    device_id_type=MESH,
                )
            )


    @pl.when(y < 3)
    def _():
        for index, d in enumerate((-1, 1, 2)):
            slot = third_of(turn(x, d), y)
            gain_copy(index, slot, partner).wait_recv()
            for way in range(3):
                copy = pltpu.make_async_remote_copy(
                    src_ref=slot,
                    dst_ref=slot,
                    send_sem=send_g.at[3 * way + index],
                    recv_sem=recv_g.at[3 * y + index],
                    device_id=y_to[way],
                    device_id_type=MESH,
                )
                copy.start()

    def drain():
        for copy in sent:
            copy.wait_send()
        for index in range(8):
            swap(index, c).wait_send()

        @pl.when(c == 0)
        def _():
            ships(True, lambda copy: copy.wait_send())

        @pl.when(c == 1)
        def _():
            ships(False, lambda copy: copy.wait_send())
            for plane in range(3):

                @pl.when(y > plane)
                def _():
                    pass_mean(plane).wait_send()

        @pl.when(y < 3)
        def _():
            for index, device in enumerate(x_to):
                gain_copy(index, third_of(x, y), device).wait_send()
            for index, d in enumerate((-1, 1, 2)):
                slot = third_of(turn(x, d), y)
                for way in range(3):
                    pltpu.make_async_remote_copy(
                        src_ref=slot,
                        dst_ref=slot,
                        send_sem=send_g.at[3 * way + index],
                        recv_sem=recv_g.at[3 * y + index],
                        device_id=y_to[way],
                        device_id_type=MESH,
                    ).wait_send()

        for index in range(3):
            gain_copy(4 + index, cg.at[c, x], partner).wait_send()
        gain_copy(3, cg.at[c, x], partner).wait_send()

    first.first_near()
    other.first_near()
    first.first_far()
    other.first_far()
    first.second_near(0)
    other.second_near(0)
    for part in range(3):

        @pl.when(y != part)
        def _():
            for index, d in enumerate((-1, 1, 2)):
                slot = third_of(turn(x, d), part)
                pltpu.make_async_remote_copy(
                    src_ref=slot,
                    dst_ref=slot,
                    send_sem=send_g.at[0],
                    recv_sem=recv_g.at[3 * part + index],
                    device_id=partner,
                    device_id_type=MESH,
                ).wait_recv()

    for index, d in enumerate((-1, 1, 2)):
        gain_copy(4 + index, cg.at[c, turn(x, d)], partner).start()

    for name in ("ret", "forc", "obs", "mn", "pm", "mix0", "mix1"):
        own[name].wait()
    for copy in small:
        copy.wait_recv()
    for place in range(4):
        for step in range(2):
            row = 2 * place + step
            ret8[pl.ds(row, 1), :] = ret4[place, pl.ds(step, 1), :]
            noise8[pl.ds(row, 1), :] = noise4[place, pl.ds(step, 1), :]
            forc16[pl.ds(row, 1), :] = forc4[place, pl.ds(step, 1), :]
            obs16[pl.ds(row, 1), :] = obs4[place, pl.ds(step, 1), :]

    gain_copy(3, cg.at[1 - c, x], partner).wait_recv()
    for index, d in enumerate((-1, 1, 2)):
        gain_copy(4 + index, cg.at[1 - c, turn(x, d)], partner).wait_recv()
    put_split(ct_h, ct_l, ..., jnp.concatenate([cg[core, place] for place in range(4) for core in range(2)], 0))
    offsets = product(forc16[...], ct_h[...], ct_l[...]) + product(obs16[...], gain_h[...], gain_l[...], True)
    off8[...] = offsets[:8]

    def swap(index, core):
        slot = gx.at[core, index]
        return pltpu.make_async_remote_copy(
            src_ref=slot,
            dst_ref=slot,
            send_sem=send_b.at[index],
            recv_sem=recv_b.at[index],
            device_id=partner,
            device_id_type=MESH,
        )

    def put_first(ks, core, value):
        high, low = split(value)
        for spot in range(4):
            target = pl.ds(pl.multiple_of(spot * 96 + core * W, 16), W)
            b_h[2 * first.s[ks], target, :] = high[W * spot : W * (spot + 1)]
            b_l[2 * first.s[ks], target, :] = low[W * spot : W * (spot + 1)]

    def put_other(ks, core, value):
        high, low = split(value)
        target = pl.ds(pl.multiple_of(other.s[ks] * 96 + core * W, 16), W)
        for spot in range(4):
            b_h[2 * spot + 1, target, :] = high[W * spot : W * (spot + 1)]
            b_l[2 * spot + 1, target, :] = low[W * spot : W * (spot + 1)]

    def kept(row, offset):
        return jnp.where(rows_of + offset == cols_of, ret8[pl.ds(row, 1), :], 0.0)

    def step_first(ks):
        place = first.s[ks]
        raw = [ga[c, place, spot] + kept(2 * place, spot * 96 + c * W) for spot in range(4)]
        value = product(jnp.concatenate(raw, 0), ct_h[...], ct_l[...])
        gx[c, ks] = value
        put_first(ks, c, value)
        swap(ks, c).start()

    def step_other(ks):
        place = other.s[ks]
        raw = [gb[c, place, spot] + kept(2 * spot + 1, place * 96 + c * W) for spot in range(4)]
        value = product(jnp.concatenate(raw, 0), ct_h[...], ct_l[...])
        gx[c, 4 + ks] = value
        put_other(ks, c, value)
        swap(4 + ks, c).start()

    def take_first(ks):
        swap(ks, 1 - c).wait_recv()
        put_first(ks, 1 - c, gx[1 - c, ks])

    def take_other(ks):
        swap(4 + ks, 1 - c).wait_recv()
        put_other(ks, 1 - c, gx[1 - c, 4 + ks])

    def ready(gather, ks):
        for kf in range(4):
            gather.shared(kf, ks)

    step_first(0)
    first.second_near(1)
    other.second_near(1)
    step_other(0)
    first.second_near(2)
    other.second_near(2)
    take_first(0)
    first.second_near(3)
    other.second_near(3)
    step_first(1)
    first.second_far(0)
    other.second_far(0)
    step_first(2)
    first.second_far(1)
    other.second_far(1)
    step_other(1)
    first.second_far(2)
    other.second_far(2)
    step_other(2)
    take_other(0)
    take_first(1)
    take_first(2)
    take_other(1)
    first.second_far(3)
    other.second_far(3)
    step_first(3)
    step_other(3)
    take_other(2)
    take_first(3)
    take_other(3)

    row32 = lax.broadcasted_iota(jnp.int32, (32, N), 0)
    col32 = lax.broadcasted_iota(jnp.int32, (32, N), 1)
    start24 = (z * 4 + x) * CR
    walk = ((row32 < CR) & (row32 + start24 == col32)).astype(F32)
    for j in range(7, -1, -1):
        wc[j] = walk
        walk = product(walk, b_h[j], b_l[j], True)
    stage[1] = walk
    mine_a, mine_b = ea.at[c, z, x], eb.at[c, x, z]

    def ship(index, source, target, slot, device):
        return pltpu.make_async_remote_copy(
            src_ref=source,
            dst_ref=target,
            send_sem=send_y.at[index],
            recv_sem=recv_y.at[slot],
            device_id=device,
            device_id_type=MESH,
        )

    def ships(first_core, act):
        near, far = pl.ds(0, 256), pl.ds(256, 128)
        if first_core:

            @pl.when(y == 1)
            def _():
                for d in range(2):
                    act(ship(d, stage.at[1, pl.ds(0, CR)], mine_a, 2, y_to[d]))

            @pl.when(y == 2)
            def _():
                act(ship(0, stage.at[1, pl.ds(0, CR)], mine_b, 3, y_to[0]))

            return
        packed, mean = stage.at[2, pl.ds(0, CR)], stage.at[0, pl.ds(CR, 8)]

        @pl.when(y == 0)
        def _():
            for d in range(3):
                act(ship(3 * d, packed.at[:, pl.ds(0, 128)], mine_a.at[:, far], 0, y_to[d]))
                act(ship(3 * d + 1, packed.at[:, pl.ds(128, 128)], mine_b.at[:, far], 1, y_to[d]))
                act(ship(3 * d + 2, mean, near_mean.at[0], 4, y_to[d]))

        @pl.when(y == 1)
        def _():
            for d in range(2):
                act(ship(2 * d, packed.at[:, near], mine_a.at[:, near], 2, y_to[d]))
                act(ship(2 * d + 1, mean, near_mean.at[1], 5, y_to[d]))

        @pl.when(y == 2)
        def _():
            act(ship(0, packed.at[:, near], mine_b.at[:, near], 3, y_to[0]))
            act(ship(1, mean, near_mean.at[2], 6, y_to[0]))

    def pass_mean(index):
        return pltpu.make_async_remote_copy(
            src_ref=near_mean.at[index],
            dst_ref=near_mean.at[index],
            send_sem=send_m.at[index],
            recv_sem=recv_m.at[index],
            device_id=partner,
            device_id_type=MESH,
        )

    @pl.when(c == 0)
    def _():
        ships(True, lambda copy: copy.start())

    @pl.when(c == 1)
    def _():
        left = wc[...].reshape(256, N)
        spread = product(left, ct_h[...], ct_l[...], True).reshape(8, 32, N) * noise8[...].reshape(8, 1, N)
        noise = product(spread.reshape(256, N), ct_h[...], ct_l[...]) + product(left, fix_h[...], fix_l[...])
        gc[...] = noise.reshape(8, 32, N)

        @pl.when(y == 0)
        def _():
            begin = product(stage[1], p_h[...], p_l[...])
            stage[0] = jnp.where(row32 == CR, pm_v[...].reshape(1, N), begin)

        @pl.when(y != 0)
        def _():
            stage[0] = jnp.zeros((32, N), F32)

        grown = stage[0]
        for j in range(8):
            grown = product(grown, b_h[j], b_l[j])
            grown = grown + gc[j] + jnp.where(row32 == CR, off8[pl.ds(j, 1), :], 0.0)
        stage[0] = grown
        band = row32[:, :128] + start24
        low, high = band < 128, band >= 256
        one, two, three = (grown[:, 128 * b : 128 * (b + 1)] for b in range(3))
        stage[2, :, pl.ds(0, 128)] = jnp.where(low, one, jnp.where(high, three, two))
        stage[2, :, pl.ds(128, 128)] = jnp.where(low, two, jnp.where(high, one, three))
        ships(False, lambda copy: copy.start())

    @pl.when((c == 0) & (y >= 2))
    def _():
        ship(0, mine_a, mine_a, 2, partner).wait_recv()

    @pl.when((c == 0) & (y >= 3))
    def _():
        ship(0, mine_b, mine_b, 3, partner).wait_recv()

    @pl.when((c == 1) & (y >= 1))
    def _():
        ship(0, mine_a.at[:, pl.ds(256, 128)], mine_a.at[:, pl.ds(256, 128)], 0, partner).wait_recv()
        ship(0, mine_b.at[:, pl.ds(256, 128)], mine_b.at[:, pl.ds(256, 128)], 1, partner).wait_recv()

    @pl.when((c == 1) & (y >= 2))
    def _():
        ship(0, mine_a.at[:, pl.ds(0, 256)], mine_a.at[:, pl.ds(0, 256)], 2, partner).wait_recv()

    @pl.when((c == 1) & (y >= 3))
    def _():
        ship(0, mine_b.at[:, pl.ds(0, 256)], mine_b.at[:, pl.ds(0, 256)], 3, partner).wait_recv()

    third = PlaneGather(lambda core, f, s: ea.at[core, s, f], CR, c, x, z, x_to, z_to, partner, send3, recv3, 0, sent, STRAIGHT3)
    fourth = PlaneGather(
        lambda core, f, s: eb.at[core, s, f], CR, c, z, x, z_to, x_to, partner, send3, recv3, PER_CLASS, sent, STRAIGHT3
    )
    for gather in (third, fourth):
        gather.first_own(gather.at(0, 0))
    for gather in (third, fourth):
        gather.first_own_far(gather.at(0, 0))
    for gather in (third, fourth):
        gather.second(0)
        gather.share(0, 0)

    for plane in range(3):

        @pl.when((c == 1) & (y > plane))
        def _():
            ship(0, near_mean.at[plane], near_mean.at[plane], 4 + plane, partner).wait_recv()
            pass_mean(plane).start()

    last = 2 * z + 1
    wf[last, pl.ds(W, W), :] = eye_rows
    behind = product(eye_rows, b_h[last], b_l[last], True)
    w0_s[pl.ds(0, W), :] = eye_rows
    w0_s[pl.ds(W, W), :] = behind

    third.first_near()
    fourth.first_near()
    third.first_far()
    fourth.first_far()

    @pl.loop(0, 2 * z + 1)
    def _(i):
        j = 2 * z - i
        rows = w0_s[...]
        wf[j] = rows
        w0_s[...] = product(rows, b_h[j], b_l[j], True)

    def noise_rows(part):
        span = pl.ds(4 * part, 4)
        rows = wf[span].reshape(N, N)
        wide = product(rows, ct_h[...], ct_l[...], True).reshape(4, 96, N)
        wide = wide * noise8[pl.ds(4 * part, 4), :].reshape(4, 1, N)
        value = product(wide.reshape(N, N), ct_h[...], ct_l[...]) + product(rows, fix_h[...], fix_l[...])
        gf[span] = value.reshape(4, 96, N)

    third.second_near(0)
    fourth.second_near(0)
    noise_rows(0)
    for kf in (1, 2):
        third.second_near(kf)
        fourth.second_near(kf)

    @pl.when(z >= 2)
    def _():
        noise_rows(1)

    third.second_near(3)
    fourth.second_near(3)
    for kf in range(4):
        third.second_far(kf)
        fourth.second_far(kf)
    for ks in range(4):
        ready(third, ks)
        ready(fourth, ks)

    spots = [(a, b) for a in range(4) for b in range(4)]

    for plane in range(3):

        @pl.when((c == 0) & (y > plane))
        def _():
            pass_mean(plane).wait_recv()

    def symmetric(own, after):
        d0, d1, d2 = (own[128 * b : 128 * (b + 1)] for b in range(3))
        u0, u1, u2 = (after[128 * b : 128 * (b + 1)] for b in range(3))
        rows = ((d0, u0, u2.T), (u0.T, d1, u1), (u2, u1.T, d2))
        return jnp.concatenate([jnp.concatenate(row, 1) for row in rows], 0)

    def columns(pick, block):
        return jnp.concatenate([pick(a, b)[:, 128 * block : 128 * (block + 1)] for a, b in spots], 0)

    def from_a(a, b):
        return ea[1, a, b]

    def from_b(a, b):
        return eb[1, b, a]

    @pl.when(y == 3)
    def _():
        put_split(t2_h, t2_l, ..., jnp.concatenate([eb[0, b, a] for a, b in spots], 0))
        put_split(n2_h, n2_l, ..., symmetric(columns(from_b, 0), columns(from_b, 1)))
        v2_s[...] = product(w0_s[...], t2_h[...], t2_l[...])

    @pl.when(y != 3)
    def _():
        v2_s[...] = w0_s[...]

    @pl.when(y >= 2)
    def _():
        put_split(t1_h, t1_l, ..., jnp.concatenate([ea[0, a, b] for a, b in spots], 0))
        put_split(n1_h, n1_l, ..., symmetric(columns(from_a, 0), columns(from_a, 1)))
        v1_s[...] = product(v2_s[...], t1_h[...], t1_l[...])

    @pl.when(y < 2)
    def _():
        v1_s[...] = v2_s[...]

    @pl.when(y >= 1)
    def _():
        put_split(p_h, p_l, ..., symmetric(columns(from_a, 2), columns(from_b, 2)))

    row16 = lax.broadcasted_iota(jnp.int32, (16, N), 0)

    def mean_rows(row):
        return jnp.where(row16 == 0, row, 0.0)

    xs[pl.ds(0, 96), :] = product(v1_s[...], p_h[...], p_l[...])

    @pl.when(y == 0)
    def _():
        xs[pl.ds(96, 16), :] = mean_rows(pm_v[...].reshape(1, N))

    @pl.when(y >= 1)
    def _():
        xs[pl.ds(96, 16), :] = mean_rows(near_mean[0, pl.ds(0, 1), :])

    @pl.when(y >= 2)
    def _():
        value = product(xs[...], t1_h[...], t1_l[...], True)
        added = product(v2_s[...], n1_h[...], n1_l[...])
        xs[...] = value + jnp.concatenate([added, mean_rows(near_mean[1, pl.ds(0, 1), :])], 0)

    @pl.when(y >= 3)
    def _():
        value = product(xs[...], t2_h[...], t2_l[...], True)
        added = product(w0_s[...], n2_h[...], n2_l[...])
        xs[...] = value + jnp.concatenate([added, mean_rows(near_mean[2, pl.ds(0, 1), :])], 0)

    @pl.loop(0, 2 * z + 1)
    def _(j):
        value = product(xs[...], b_h[j], b_l[j])
        xs[...] = value + jnp.concatenate([gf[j], mean_rows(off8[pl.ds(j, 1), :])], 0)

    covariances[0] = xs[pl.ds(0, W), :]
    means[pl.ds(0, 1), :] = xs[pl.ds(96, 1), :]
    value = product(xs[pl.ds(W, 64), :], b_h[last], b_l[last])
    covariances[1] = value[:W] + gf[last, pl.ds(W, W), :]
    means[pl.ds(1, 1), :] = value[W : W + 1] + off8[pl.ds(last, 1), :]
    drain()


def finish(near_means, near_covariances, means, covariances, done):
    copies = [
        pltpu.make_async_copy(near_means, means, done.at[0]),
        pltpu.make_async_copy(near_covariances, covariances, done.at[1]),
    ]
    for copy in copies:
        copy.start()
    for copy in copies:
        copy.wait()


def vmem(shape, dtype=F32):
    return pltpu.VMEM(shape, dtype)


def pair(shape):
    return [vmem(shape, BF16), vmem(shape, BF16)]


def per_device(mixing, retention, forcing, observations, model_noise, obs_noise, gain, obs_t, prior_mean, prior_factor):
    dma = pltpu.SemaphoreType.DMA
    square = (N, N)
    near = pl.pallas_call(
        kernel,
        out_shape=(pltpu.VMEM((2, N), F32), pltpu.VMEM((2, W, N), F32)),
        in_specs=[pl.BlockSpec(memory_space=pltpu.HBM)] * 10,
        out_specs=(pl.BlockSpec(memory_space=pltpu.VMEM),) * 2,
        scratch_shapes=[
            vmem((2, 4, 4, W, N)),
            vmem((2, 4, 4, W, N)),
            vmem((2, 8, 4 * W, N)),
            vmem((2, 4, W, N)),
            vmem((2, 4, 4, CR, N)),
            vmem((2, 4, 4, CR, N)),
            vmem((4, 2, N)),
            vmem((4, 2, N)),
            vmem((4, 2, NOBS)),
            vmem((4, 2, N)),
            vmem((8, N)),
            vmem((16, N)),
            vmem((16, NOBS)),
            vmem((8, N)),
            vmem((1, NOBS)),
            vmem((N, NOBS)),
            *pair((N, NOBS)),
            vmem((W, NOBS)),
            vmem((N,)),
            vmem(square),
            *pair(square),
            *pair(square),
            *pair(square),
            *pair((8, N, N)),
            vmem((8, N)),
            vmem((8, 32, N)),
            vmem((8, 32, N)),
            vmem((8, 96, N)),
            vmem((8, 96, N)),
            vmem((3, 32, N)),
            vmem((3, 8, N)),
            *pair(square),
            *pair(square),
            *pair(square),
            *pair(square),
            vmem((96, N)),
            vmem((96, N)),
            vmem((96, N)),
            vmem((112, N)),
            dma((2 * PER_CLASS,)),
            dma((2 * PER_CLASS,)),
            dma((2 * PER_CLASS,)),
            dma((2 * PER_CLASS,)),
            dma((7,)),
            dma((7,)),
            dma((9,)),
            dma((9,)),
            dma((12,)),
            dma((12,)),
            dma((9,)),
            dma((7,)),
            dma((3,)),
            dma((3,)),
            dma((8,)),
            dma((8,)),
            dma((11,)),
        ],
        compiler_params=pltpu.CompilerParams(
            collective_id=0, has_side_effects=True, vmem_limit_bytes=60 * 1024 * 1024
        ),
        name="prefix",
    )(
        mixing, retention, forcing, observations, model_noise, obs_noise.reshape(1, NOBS), gain, obs_t,
        prior_mean, prior_factor,
    )
    return pl.pallas_call(
        finish,
        out_shape=(jax.ShapeDtypeStruct((2, N), F32), jax.ShapeDtypeStruct((2, W, N), F32)),
        in_specs=[pl.BlockSpec(memory_space=pltpu.VMEM)] * 2,
        out_specs=(pl.BlockSpec(memory_space=pltpu.HBM),) * 2,
        scratch_shapes=[pltpu.SemaphoreType.DMA((2,))],
        compiler_params=pltpu.CompilerParams(vmem_limit_bytes=1024 * 1024),
        name="finish",
    )(*near)


def solution(mesh):
    grid = Mesh(mesh.devices.reshape(4, 4, 4, 2), SEG + COL)
    placed = (
        P(SEG, COL, None),
        P(SEG, None),
        P(SEG, None),
        P(SEG, None),
        P(SEG, None),
        P(),
        P(),
        P(COL, None),
        P(),
        P(),
    )
    return jax.shard_map(
        per_device,
        mesh=grid,
        in_specs=placed,
        out_specs=(P(SEG, None), P(SEG, COL, None)),
        check_vma=False,
    )
```

```python
import functools

import jax
import jax.numpy as jnp
from jax import lax
from jax.experimental import pallas as pl
from jax.experimental.pallas import tpu as pltpu
from jax.sharding import Mesh
from jax.sharding import PartitionSpec as P

MESH = pl.DeviceIdType.MESH
F32 = jnp.float32
BF16 = jnp.bfloat16
SEG = ("y", "z")
COL = ("x", "c")
N = 384
NOBS = 1024
W = 48
CR = 24
PER_CLASS = 36
STRAIGHT1 = (3,)
STRAIGHT3 = (0, 1, 2, 3)


def split(value):
    high = value.astype(BF16)
    low = (value - high.astype(F32)).astype(BF16)
    return high, low


def dot(left, right, transposed):
    dims = (((1,), (1 if transposed else 0,)), ((), ()))
    return lax.dot_general(left, right, dims, preferred_element_type=F32)


def product(left, right_high, right_low, transposed=False):
    high, low = split(left)
    rows = left.shape[0]
    both = dot(jnp.concatenate([high, low], 0), right_high, transposed)
    return both[:rows] + (both[rows:] + dot(high, right_low, transposed))


def put_split(high_ref, low_ref, index, value):
    high, low = split(value)
    high_ref[index] = high
    low_ref[index] = low


def turn(position, by):
    return lax.rem(position + (by % 4), 4)


class PlaneGather:
    def __init__(self, unit, rows, core, first, second, to_first, to_second, partner, send, recv, base, sent, straight, sharing=True):
        self.unit, self.rows, self.core = unit, rows, core
        self.f = [turn(first, d) for d in (0, -1, 1, 2)]
        self.s = [turn(second, d) for d in (0, -1, 1, 2)]
        self.to_first, self.to_second, self.partner = to_first, to_second, partner
        self.send, self.recv, self.base, self.sent, self.straight = send, recv, base, sent, straight
        self.sharing = sharing

    def at(self, kf, ks, half=None, core=None):
        ref = self.unit(self.core if core is None else core, self.f[kf], self.s[ks])
        if half is None:
            return ref
        middle = self.rows // 16 * 8
        return ref.at[pl.ds(0, middle)] if half == 0 else ref.at[pl.ds(middle, self.rows - middle)]

    def start(self, index, source, target, device):
        copy = pltpu.make_async_remote_copy(
            src_ref=source,
            dst_ref=target,
            send_sem=self.send.at[self.base + index],
            recv_sem=self.recv.at[self.base + index],
            device_id=device,
            device_id_type=MESH,
        )
        copy.start()
        self.sent.append(copy)

    def arrive(self, index, slot):
        pltpu.make_async_remote_copy(
            src_ref=slot,
            dst_ref=slot,
            send_sem=self.send.at[self.base + index],
            recv_sem=self.recv.at[self.base + index],
            device_id=self.partner,
            device_id_type=MESH,
        ).wait_recv()

    def first_own(self, source):
        for way in (0, 1):
            self.start(way, source, self.at(0, 0), self.to_first[way])

    def first_own_far(self, source):
        self.start(2, source, self.at(0, 0), self.to_first[2])

    def share(self, kf, ks, source=None):
        if not self.sharing:
            return
        slot = self.at(kf, ks)
        self.start(20 + 4 * ks + kf, slot if source is None else source, slot, self.partner)

    def shared(self, kf, ks):
        self.arrive(20 + 4 * ks + kf, self.at(kf, ks, core=1 - self.core))

    def second(self, kf, source=None):
        slot = self.at(kf, 0)
        source = slot if source is None else source
        for way in (0, 1):
            self.start(4 + 2 * kf + way, source, slot, self.to_second[way])
        if kf in self.straight:
            self.start(12 + 2 * kf, source, slot, self.to_second[2])

    def first_near(self):
        for way in (0, 1):
            self.arrive(way, self.at(1 + way, 0))
            self.second(1 + way)
            self.share(1 + way, 0)

    def first_far(self):
        self.arrive(2, self.at(3, 0))
        self.second(3)
        self.share(3, 0)

    def second_near(self, kf):
        for way in (0, 1):
            self.arrive(4 + 2 * kf + way, self.at(kf, 1 + way))
            if kf not in self.straight:
                part = self.at(kf, 1 + way, half=way)
                self.start(12 + 2 * kf + way, part, part, self.to_second[way])
            self.share(kf, 1 + way)

    def second_far(self, kf):
        if kf in self.straight:
            self.arrive(12 + 2 * kf, self.at(kf, 3))
        else:
            for way in (0, 1):
                self.arrive(12 + 2 * kf + way, self.at(kf, 3, half=way))
        self.share(kf, 3)


def kernel(
    mixing, retention, forcing, observations, model_noise, obs_noise, gain, obs_t, prior_mean, prior_factor,
    means, covariances,
    ga, gb, gx, cg, ea, eb, ret4, forc4, obs4, noise4, ret8, forc16, obs16, noise8, on_v, gain_v, gain_h, gain_l,
    obs_v, pm_v, pf_v, ct_h, ct_l, fix_h, fix_l, p_h, p_l, b_h, b_l, off8, wc, gc, wf, gf, stage,
    near_mean, t1_h, t1_l, n1_h, n1_l, t2_h, t2_l, n2_h, n2_l, w0_s, v1_s, v2_s, xs, nz, ph_f, ph_h, ph_l,
    send1, recv1, send3, recv3, send_c, recv_c, send_g, recv_g, send_s, recv_s, send_y, recv_y, send_m, recv_m, send_b, recv_b, local,
):
    y, z, x, c = (lax.axis_index(name) for name in ("y", "z", "x", "c"))
    partner = (y, z, x, 1 - c)
    x_to = [(y, z, turn(x, d), c) for d in (1, -1, 2)]
    z_to = [(y, turn(z, d), x, c) for d in (1, -1, 2)]
    y_to = [(turn(y, d), z, x, c) for d in (1, 2, 3)]
    sent = []

    own = {}
    for index, (name, source, target) in enumerate(
        (
            ("gain", gain, gain_v),
            ("obs_t", obs_t, obs_v),
            ("mix0", mixing.at[0], ga.at[c, z, x]),
            ("mix1", mixing.at[1], gb.at[c, x, z]),
            ("noise", obs_noise, on_v),
            ("ret", retention, ret4.at[z]),
            ("forc", forcing, forc4.at[z]),
            ("obs", observations, obs4.at[z]),
            ("mn", model_noise, noise4.at[z]),
            ("pm", prior_mean, pm_v),
            ("pf", prior_factor, pf_v),
        )
    ):
        own[name] = pltpu.make_async_copy(source, target, local.at[index])
        own[name].start()

    ea[c, z, x] = jnp.zeros((CR, N), F32)
    eb[c, x, z] = jnp.zeros((CR, N), F32)
    forc16[...] = jnp.zeros((16, N), F32)
    obs16[...] = jnp.zeros((16, NOBS), F32)

    barrier = pltpu.get_barrier_semaphore()
    friends = [partner] + x_to + z_to + y_to
    for friend in friends:
        pl.semaphore_signal(barrier, inc=1, device_id=friend, device_id_type=MESH)

    own["gain"].wait()
    own["obs_t"].wait()
    own["noise"].wait()
    put_split(gain_h, gain_l, ..., gain_v[...])
    rows_of = lax.broadcasted_iota(jnp.int32, (W, N), 0)
    cols_of = lax.broadcasted_iota(jnp.int32, (W, N), 1)
    start_row = x * 96 + c * W
    eye_rows = (rows_of + start_row == cols_of).astype(F32)
    cg[c, x] = eye_rows - product(obs_v[...], gain_h[...], gain_l[...], True)
    for part in range(3):
        rows = pl.ds(part * 128, 128)
        put_split(fix_h, fix_l, rows, product(gain_v[rows, :] * on_v[...], gain_h[...], gain_l[...], True))

    own["pf"].wait()

    @pl.when(y == 0)
    def _():
        high, low = split(pf_v[...])
        put_split(p_h, p_l, ..., product(pf_v[...], high, low, True))

    pl.semaphore_wait(barrier, len(friends))

    first = PlaneGather(lambda core, f, s: ga.at[core, s, f], W, c, x, z, x_to, z_to, partner, send1, recv1, 0, sent, STRAIGHT1, False)
    other = PlaneGather(
        lambda core, f, s: gb.at[core, s, f], W, c, z, x, z_to, x_to, partner, send1, recv1, PER_CLASS, sent, STRAIGHT1, False
    )

    def gain_copy(index, slot, device):
        return pltpu.make_async_remote_copy(
            src_ref=slot,
            dst_ref=slot,
            send_sem=send_c.at[index],
            recv_sem=recv_c.at[index],
            device_id=device,
            device_id_type=MESH,
        )

    def third_of(place, part):
        return cg.at[c, place, pl.ds(16 * part, 16)]

    @pl.when(y < 3)
    def _():
        for index, device in enumerate(x_to):
            gain_copy(index, third_of(x, y), device).start()

    for gather, step in ((first, 0), (other, 1)):
        gather.first_own(mixing.at[step])
    for gather, step in ((first, 0), (other, 1)):
        gather.first_own_far(mixing.at[step])
    for gather, step in ((first, 0), (other, 1)):
        gather.second(0, mixing.at[step])
    gain_copy(3, cg.at[c, x], partner).start()
    for gather, step in ((first, 0), (other, 1)):
        gather.share(0, 0, mixing.at[step])

    small = []
    for array, (source, target) in enumerate(
        ((retention, ret4), (forcing, forc4), (observations, obs4), (model_noise, noise4))
    ):
        for d in (1, 2, 3):
            index = 3 * array + d - 1
            copy = pltpu.make_async_remote_copy(
                src_ref=source,
                dst_ref=target.at[z],
                send_sem=send_s.at[index],
                recv_sem=recv_s.at[index],
                device_id=(y, turn(z, d), x, c),
                device_id_type=MESH,
            )
            copy.start()
            sent.append(copy)
            slot = target.at[turn(z, -d)]
            small.append(
                pltpu.make_async_remote_copy(
                    src_ref=slot,
                    dst_ref=slot,
                    send_sem=send_s.at[index],
                    recv_sem=recv_s.at[index],
                    device_id=partner,
                    device_id_type=MESH,
                )
            )


    @pl.when(y < 3)
    def _():
        for index, d in enumerate((-1, 1, 2)):
            slot = third_of(turn(x, d), y)
            gain_copy(index, slot, partner).wait_recv()
            for way in range(3):
                copy = pltpu.make_async_remote_copy(
                    src_ref=slot,
                    dst_ref=slot,
                    send_sem=send_g.at[3 * way + index],
                    recv_sem=recv_g.at[3 * y + index],
                    device_id=y_to[way],
                    device_id_type=MESH,
                )
                copy.start()

    def drain():
        for copy in sent:
            copy.wait_send()
        for index in range(8):
            swap(index, c).wait_send()
        swap_phi(c).wait_send()

        @pl.when(c == 0)
        def _():
            ships(True, lambda copy: copy.wait_send())

        @pl.when(c == 1)
        def _():
            ships(False, lambda copy: copy.wait_send())
            for plane in range(3):

                @pl.when(y > plane)
                def _():
                    pass_mean(plane).wait_send()

        @pl.when(y < 3)
        def _():
            for index, device in enumerate(x_to):
                gain_copy(index, third_of(x, y), device).wait_send()
            for index, d in enumerate((-1, 1, 2)):
                slot = third_of(turn(x, d), y)
                for way in range(3):
                    pltpu.make_async_remote_copy(
                        src_ref=slot,
                        dst_ref=slot,
                        send_sem=send_g.at[3 * way + index],
                        recv_sem=recv_g.at[3 * y + index],
                        device_id=y_to[way],
                        device_id_type=MESH,
                    ).wait_send()

        for index in range(3):
            gain_copy(4 + index, cg.at[c, x], partner).wait_send()
        gain_copy(3, cg.at[c, x], partner).wait_send()

    first.first_near()
    other.first_near()
    first.first_far()
    other.first_far()
    first.second_near(0)
    other.second_near(0)
    for part in range(3):

        @pl.when(y != part)
        def _():
            for index, d in enumerate((-1, 1, 2)):
                slot = third_of(turn(x, d), part)
                pltpu.make_async_remote_copy(
                    src_ref=slot,
                    dst_ref=slot,
                    send_sem=send_g.at[0],
                    recv_sem=recv_g.at[3 * part + index],
                    device_id=partner,
                    device_id_type=MESH,
                ).wait_recv()

    for index, d in enumerate((-1, 1, 2)):
        gain_copy(4 + index, cg.at[c, turn(x, d)], partner).start()

    for name in ("ret", "forc", "obs", "mn", "pm", "mix0", "mix1"):
        own[name].wait()
    for copy in small:
        copy.wait_recv()
    for place in range(4):
        for step in range(2):
            row = 2 * place + step
            ret8[pl.ds(row, 1), :] = ret4[place, pl.ds(step, 1), :]
            noise8[pl.ds(row, 1), :] = noise4[place, pl.ds(step, 1), :]
            forc16[pl.ds(row, 1), :] = forc4[place, pl.ds(step, 1), :]
            obs16[pl.ds(row, 1), :] = obs4[place, pl.ds(step, 1), :]

    gain_copy(3, cg.at[1 - c, x], partner).wait_recv()
    for index, d in enumerate((-1, 1, 2)):
        gain_copy(4 + index, cg.at[1 - c, turn(x, d)], partner).wait_recv()
    put_split(ct_h, ct_l, ..., jnp.concatenate([cg[core, place] for place in range(4) for core in range(2)], 0))
    offsets = product(forc16[...], ct_h[...], ct_l[...]) + product(obs16[...], gain_h[...], gain_l[...], True)
    off8[...] = offsets[:8]

    def swap(index, core):
        slot = gx.at[core, index]
        return pltpu.make_async_remote_copy(
            src_ref=slot,
            dst_ref=slot,
            send_sem=send_b.at[index],
            recv_sem=recv_b.at[index],
            device_id=partner,
            device_id_type=MESH,
        )

    def put_first(ks, core, value):
        high, low = split(value)
        for spot in range(4):
            target = pl.ds(pl.multiple_of(spot * 96 + core * W, 16), W)
            b_h[2 * first.s[ks], target, :] = high[W * spot : W * (spot + 1)]
            b_l[2 * first.s[ks], target, :] = low[W * spot : W * (spot + 1)]

    def put_other(ks, core, value):
        high, low = split(value)
        target = pl.ds(pl.multiple_of(other.s[ks] * 96 + core * W, 16), W)
        for spot in range(4):
            b_h[2 * spot + 1, target, :] = high[W * spot : W * (spot + 1)]
            b_l[2 * spot + 1, target, :] = low[W * spot : W * (spot + 1)]

    def kept(row, offset):
        return jnp.where(rows_of + offset == cols_of, ret8[pl.ds(row, 1), :], 0.0)

    def step_first(ks):
        place = first.s[ks]
        raw = [ga[c, place, spot] + kept(2 * place, spot * 96 + c * W) for spot in range(4)]
        value = product(jnp.concatenate(raw, 0), ct_h[...], ct_l[...])
        gx[c, ks] = value
        put_first(ks, c, value)
        swap(ks, c).start()

    def step_other(ks):
        place = other.s[ks]
        raw = [gb[c, place, spot] + kept(2 * spot + 1, place * 96 + c * W) for spot in range(4)]
        value = product(jnp.concatenate(raw, 0), ct_h[...], ct_l[...])
        gx[c, 4 + ks] = value
        put_other(ks, c, value)
        swap(4 + ks, c).start()

    def take_first(ks):
        swap(ks, 1 - c).wait_recv()
        put_first(ks, 1 - c, gx[1 - c, ks])

    def take_other(ks):
        swap(4 + ks, 1 - c).wait_recv()
        put_other(ks, 1 - c, gx[1 - c, 4 + ks])

    def ready(gather, ks):
        for kf in range(4):
            gather.shared(kf, ks)

    step_first(0)
    first.second_near(1)
    other.second_near(1)
    step_other(0)
    first.second_near(2)
    other.second_near(2)
    take_first(0)
    first.second_near(3)
    other.second_near(3)
    step_first(1)
    first.second_far(0)
    other.second_far(0)
    step_first(2)
    first.second_far(1)
    other.second_far(1)
    step_other(1)
    first.second_far(2)
    other.second_far(2)
    step_other(2)
    take_other(0)
    take_first(1)
    take_first(2)
    take_other(1)
    first.second_far(3)
    other.second_far(3)
    step_first(3)
    step_other(3)
    take_other(2)
    take_first(3)
    take_other(3)

    row32 = lax.broadcasted_iota(jnp.int32, (32, N), 0)
    col32 = lax.broadcasted_iota(jnp.int32, (32, N), 1)
    start24 = (z * 4 + x) * CR
    walk = ((row32 < CR) & (row32 + start24 == col32)).astype(F32)
    for j in range(7, -1, -1):
        wc[j] = walk
        walk = product(walk, b_h[j], b_l[j], True)
    stage[1] = walk
    mine_a, mine_b = ea.at[c, z, x], eb.at[c, x, z]

    def ship(index, source, target, slot, device):
        return pltpu.make_async_remote_copy(
            src_ref=source,
            dst_ref=target,
            send_sem=send_y.at[index],
            recv_sem=recv_y.at[slot],
            device_id=device,
            device_id_type=MESH,
        )

    def ships(first_core, act):
        near, far = pl.ds(0, 256), pl.ds(256, 128)
        if first_core:

            @pl.when(y == 1)
            def _():
                for d in range(2):
                    act(ship(d, stage.at[1, pl.ds(0, CR)], mine_a, 2, y_to[d]))

            @pl.when(y == 2)
            def _():
                act(ship(0, stage.at[1, pl.ds(0, CR)], mine_b, 3, y_to[0]))

            return
        packed, mean = stage.at[2, pl.ds(0, CR)], stage.at[0, pl.ds(CR, 8)]

        @pl.when(y == 0)
        def _():
            for d in range(3):
                act(ship(3 * d, packed.at[:, pl.ds(0, 128)], mine_a.at[:, far], 0, y_to[d]))
                act(ship(3 * d + 1, packed.at[:, pl.ds(128, 128)], mine_b.at[:, far], 1, y_to[d]))
                act(ship(3 * d + 2, mean, near_mean.at[0], 4, y_to[d]))

        @pl.when(y == 1)
        def _():
            for d in range(2):
                act(ship(2 * d, packed.at[:, near], mine_a.at[:, near], 2, y_to[d]))
                act(ship(2 * d + 1, mean, near_mean.at[1], 5, y_to[d]))

        @pl.when(y == 2)
        def _():
            act(ship(0, packed.at[:, near], mine_b.at[:, near], 3, y_to[0]))
            act(ship(1, mean, near_mean.at[2], 6, y_to[0]))

    def pass_mean(index):
        return pltpu.make_async_remote_copy(
            src_ref=near_mean.at[index],
            dst_ref=near_mean.at[index],
            send_sem=send_m.at[index],
            recv_sem=recv_m.at[index],
            device_id=partner,
            device_id_type=MESH,
        )

    @pl.when(c == 0)
    def _():
        ships(True, lambda copy: copy.start())

    @pl.when(c == 1)
    def _():
        left = wc[...].reshape(256, N)
        spread = product(left, ct_h[...], ct_l[...], True).reshape(8, 32, N) * noise8[...].reshape(8, 1, N)
        noise = product(spread.reshape(256, N), ct_h[...], ct_l[...]) + product(left, fix_h[...], fix_l[...])
        gc[...] = noise.reshape(8, 32, N)

        @pl.when(y == 0)
        def _():
            begin = product(stage[1], p_h[...], p_l[...])
            stage[0] = jnp.where(row32 == CR, pm_v[...].reshape(1, N), begin)

        @pl.when(y != 0)
        def _():
            stage[0] = jnp.zeros((32, N), F32)

        grown = stage[0]
        for j in range(8):
            grown = product(grown, b_h[j], b_l[j])
            grown = grown + gc[j] + jnp.where(row32 == CR, off8[pl.ds(j, 1), :], 0.0)
        stage[0] = grown
        band = row32[:, :128] + start24
        low, high = band < 128, band >= 256
        one, two, three = (grown[:, 128 * b : 128 * (b + 1)] for b in range(3))
        stage[2, :, pl.ds(0, 128)] = jnp.where(low, one, jnp.where(high, three, two))
        stage[2, :, pl.ds(128, 128)] = jnp.where(low, two, jnp.where(high, one, three))
        ships(False, lambda copy: copy.start())

    last = 2 * z + 1
    wf[last, pl.ds(W, W), :] = eye_rows
    behind = product(eye_rows, b_h[last], b_l[last], True)
    w0_s[pl.ds(0, W), :] = eye_rows
    w0_s[pl.ds(W, W), :] = behind

    @pl.loop(0, 2 * z + 1)
    def _(i):
        j = 2 * z - i
        rows = w0_s[...]
        wf[j] = rows
        w0_s[...] = product(rows, b_h[j], b_l[j], True)

    def noise_rows(part):
        span = pl.ds(4 * part, 4)
        rows = wf[span].reshape(N, N)
        wide = product(rows, ct_h[...], ct_l[...], True).reshape(4, 96, N)
        wide = wide * noise8[pl.ds(4 * part, 4), :].reshape(4, 1, N)
        value = product(wide.reshape(N, N), ct_h[...], ct_l[...]) + product(rows, fix_h[...], fix_l[...])
        gf[span] = value.reshape(4, 96, N)


    @pl.when((c == 0) & (y >= 2))
    def _():
        ship(0, mine_a, mine_a, 2, partner).wait_recv()

    @pl.when((c == 0) & (y >= 3))
    def _():
        ship(0, mine_b, mine_b, 3, partner).wait_recv()

    @pl.when((c == 1) & (y >= 1))
    def _():
        ship(0, mine_a.at[:, pl.ds(256, 128)], mine_a.at[:, pl.ds(256, 128)], 0, partner).wait_recv()
        ship(0, mine_b.at[:, pl.ds(256, 128)], mine_b.at[:, pl.ds(256, 128)], 1, partner).wait_recv()

    @pl.when((c == 1) & (y >= 2))
    def _():
        ship(0, mine_a.at[:, pl.ds(0, 256)], mine_a.at[:, pl.ds(0, 256)], 2, partner).wait_recv()

    @pl.when((c == 1) & (y >= 3))
    def _():
        ship(0, mine_b.at[:, pl.ds(0, 256)], mine_b.at[:, pl.ds(0, 256)], 3, partner).wait_recv()

    third = PlaneGather(lambda core, f, s: ea.at[core, s, f], CR, c, x, z, x_to, z_to, partner, send3, recv3, 0, sent, STRAIGHT3)
    fourth = PlaneGather(
        lambda core, f, s: eb.at[core, s, f], CR, c, z, x, z_to, x_to, partner, send3, recv3, PER_CLASS, sent, STRAIGHT3
    )
    for gather in (third, fourth):
        gather.first_own(gather.at(0, 0))
    for gather in (third, fourth):
        gather.first_own_far(gather.at(0, 0))
    for gather in (third, fourth):
        gather.second(0)
        gather.share(0, 0)

    for plane in range(3):

        @pl.when((c == 1) & (y > plane))
        def _():
            ship(0, near_mean.at[plane], near_mean.at[plane], 4 + plane, partner).wait_recv()
            pass_mean(plane).start()

    own_half = pl.ds(pl.multiple_of(c * 192, 64), 192)
    ph_f[c] = b_h[0, own_half, :].astype(F32) + b_l[0, own_half, :].astype(F32)

    @pl.loop(1, 2 * z + 1)
    def _(j):
        ph_f[c] = product(ph_f[c], b_h[j], b_l[j])

    def swap_phi(core):
        slot = ph_f.at[core]
        return pltpu.make_async_remote_copy(
            src_ref=slot,
            dst_ref=slot,
            send_sem=send_b.at[8],
            recv_sem=recv_b.at[8],
            device_id=partner,
            device_id_type=MESH,
        )

    third.first_near()
    fourth.first_near()
    third.first_far()
    fourth.first_far()
    swap_phi(c).start()
    noise_rows(0)

    third.second_near(0)
    fourth.second_near(0)

    @pl.when(z >= 2)
    def _():
        noise_rows(1)

    for kf in (1, 2):
        third.second_near(kf)
        fourth.second_near(kf)

    row16 = lax.broadcasted_iota(jnp.int32, (16, N), 0)

    def mean_rows(row):
        return jnp.where(row16 == 0, row, 0.0)

    def fresh(j):
        return jnp.concatenate([gf[j], mean_rows(off8[pl.ds(j, 1), :])], 0)

    nz[...] = fresh(0)

    @pl.loop(1, z + 1)
    def _(j):
        nz[...] = product(nz[...], b_h[j], b_l[j]) + fresh(j)

    third.second_near(3)
    fourth.second_near(3)

    @pl.loop(z + 1, 2 * z + 1)
    def _(j):
        nz[...] = product(nz[...], b_h[j], b_l[j]) + fresh(j)

    swap_phi(1 - c).wait_recv()
    for core in range(2):
        high, low = split(ph_f[core])
        ph_h[pl.ds(192 * core, 192), :] = high
        ph_l[pl.ds(192 * core, 192), :] = low

    spots = [(a, b) for a in range(4) for b in range(4)]

    def symmetric(own, after):
        d0, d1, d2 = (own[128 * b : 128 * (b + 1)] for b in range(3))
        u0, u1, u2 = (after[128 * b : 128 * (b + 1)] for b in range(3))
        rows = ((d0, u0, u2.T), (u0.T, d1, u1), (u2, u1.T, d2))
        return jnp.concatenate([jnp.concatenate(row, 1) for row in rows], 0)

    def columns(pick, block):
        return jnp.concatenate([pick(a, b)[:, 128 * block : 128 * (block + 1)] for a, b in spots], 0)

    def from_a(a, b):
        return ea[1, a, b]

    def from_b(a, b):
        return eb[1, b, a]

    def ready_all():
        for ks in range(4):
            ready(third, ks)
            ready(fourth, ks)

    def prepare_steps():
        @pl.when(y == 3)
        def _():
            put_split(t2_h, t2_l, ..., jnp.concatenate([eb[0, b, a] for a, b in spots], 0))
            v2_s[...] = product(w0_s[...], t2_h[...], t2_l[...])

        @pl.when(y != 3)
        def _():
            v2_s[...] = w0_s[...]

        @pl.when(y >= 2)
        def _():
            put_split(t1_h, t1_l, ..., jnp.concatenate([ea[0, a, b] for a, b in spots], 0))
            v1_s[...] = product(v2_s[...], t1_h[...], t1_l[...])

        @pl.when(y < 2)
        def _():
            v1_s[...] = v2_s[...]

    for kf in range(4):
        third.second_far(kf)
        fourth.second_far(kf)

    @pl.when(c == 0)
    def _():
        prepare_steps()
        ready_all()

    @pl.when(c == 1)
    def _():
        ready_all()
        prepare_steps()

    for plane in range(3):

        @pl.when((c == 0) & (y > plane))
        def _():
            pass_mean(plane).wait_recv()

    @pl.when(y >= 1)
    def _():
        put_split(p_h, p_l, ..., symmetric(columns(from_a, 2), columns(from_b, 2)))

    @pl.when(y >= 2)
    def _():
        put_split(n1_h, n1_l, ..., symmetric(columns(from_a, 0), columns(from_a, 1)))

    @pl.when(y == 3)
    def _():
        put_split(n2_h, n2_l, ..., symmetric(columns(from_b, 0), columns(from_b, 1)))

    xs[pl.ds(0, 96), :] = product(v1_s[...], p_h[...], p_l[...])

    @pl.when(y == 0)
    def _():
        xs[pl.ds(96, 16), :] = mean_rows(pm_v[...].reshape(1, N))

    @pl.when(y >= 1)
    def _():
        xs[pl.ds(96, 16), :] = mean_rows(near_mean[0, pl.ds(0, 1), :])

    @pl.when(y >= 2)
    def _():
        value = product(xs[...], t1_h[...], t1_l[...], True)
        added = product(v2_s[...], n1_h[...], n1_l[...])
        xs[...] = value + jnp.concatenate([added, mean_rows(near_mean[1, pl.ds(0, 1), :])], 0)

    @pl.when(y >= 3)
    def _():
        value = product(xs[...], t2_h[...], t2_l[...], True)
        added = product(w0_s[...], n2_h[...], n2_l[...])
        xs[...] = value + jnp.concatenate([added, mean_rows(near_mean[2, pl.ds(0, 1), :])], 0)

    xs[...] = product(xs[...], ph_h[...], ph_l[...]) + nz[...]

    covariances[0] = xs[pl.ds(0, W), :]
    means[pl.ds(0, 1), :] = xs[pl.ds(96, 1), :]
    value = product(xs[pl.ds(W, 64), :], b_h[last], b_l[last])
    covariances[1] = value[:W] + gf[last, pl.ds(W, W), :]
    means[pl.ds(1, 1), :] = value[W : W + 1] + off8[pl.ds(last, 1), :]
    drain()


def finish(near_means, near_covariances, means, covariances, done):
    copies = [
        pltpu.make_async_copy(near_means, means, done.at[0]),
        pltpu.make_async_copy(near_covariances, covariances, done.at[1]),
    ]
    for copy in copies:
        copy.start()
    for copy in copies:
        copy.wait()


def vmem(shape, dtype=F32):
    return pltpu.VMEM(shape, dtype)


def pair(shape):
    return [vmem(shape, BF16), vmem(shape, BF16)]


def per_device(mixing, retention, forcing, observations, model_noise, obs_noise, gain, obs_t, prior_mean, prior_factor):
    dma = pltpu.SemaphoreType.DMA
    square = (N, N)
    near = pl.pallas_call(
        kernel,
        out_shape=(pltpu.VMEM((2, N), F32), pltpu.VMEM((2, W, N), F32)),
        in_specs=[pl.BlockSpec(memory_space=pltpu.HBM)] * 10,
        out_specs=(pl.BlockSpec(memory_space=pltpu.VMEM),) * 2,
        scratch_shapes=[
            vmem((2, 4, 4, W, N)),
            vmem((2, 4, 4, W, N)),
            vmem((2, 8, 4 * W, N)),
            vmem((2, 4, W, N)),
            vmem((2, 4, 4, CR, N)),
            vmem((2, 4, 4, CR, N)),
            vmem((4, 2, N)),
            vmem((4, 2, N)),
            vmem((4, 2, NOBS)),
            vmem((4, 2, N)),
            vmem((8, N)),
            vmem((16, N)),
            vmem((16, NOBS)),
            vmem((8, N)),
            vmem((1, NOBS)),
            vmem((N, NOBS)),
            *pair((N, NOBS)),
            vmem((W, NOBS)),
            vmem((N,)),
            vmem(square),
            *pair(square),
            *pair(square),
            *pair(square),
            *pair((8, N, N)),
            vmem((8, N)),
            vmem((8, 32, N)),
            vmem((8, 32, N)),
            vmem((8, 96, N)),
            vmem((8, 96, N)),
            vmem((3, 32, N)),
            vmem((3, 8, N)),
            *pair(square),
            *pair(square),
            *pair(square),
            *pair(square),
            vmem((96, N)),
            vmem((96, N)),
            vmem((96, N)),
            vmem((112, N)),
            vmem((112, N)),
            vmem((2, 192, N)),
            *pair(square),
            dma((2 * PER_CLASS,)),
            dma((2 * PER_CLASS,)),
            dma((2 * PER_CLASS,)),
            dma((2 * PER_CLASS,)),
            dma((7,)),
            dma((7,)),
            dma((9,)),
            dma((9,)),
            dma((12,)),
            dma((12,)),
            dma((9,)),
            dma((7,)),
            dma((3,)),
            dma((3,)),
            dma((9,)),
            dma((9,)),
            dma((11,)),
        ],
        compiler_params=pltpu.CompilerParams(
            collective_id=0, has_side_effects=True, vmem_limit_bytes=60 * 1024 * 1024
        ),
        name="prefix",
    )(
        mixing, retention, forcing, observations, model_noise, obs_noise.reshape(1, NOBS), gain, obs_t,
        prior_mean, prior_factor,
    )
    return pl.pallas_call(
        finish,
        out_shape=(jax.ShapeDtypeStruct((2, N), F32), jax.ShapeDtypeStruct((2, W, N), F32)),
        in_specs=[pl.BlockSpec(memory_space=pltpu.VMEM)] * 2,
        out_specs=(pl.BlockSpec(memory_space=pltpu.HBM),) * 2,
        scratch_shapes=[pltpu.SemaphoreType.DMA((2,))],
        compiler_params=pltpu.CompilerParams(vmem_limit_bytes=1024 * 1024),
        name="finish",
    )(*near)


def solution(mesh):
    grid = Mesh(mesh.devices.reshape(4, 4, 4, 2), SEG + COL)
    placed = (
        P(SEG, COL, None),
        P(SEG, None),
        P(SEG, None),
        P(SEG, None),
        P(SEG, None),
        P(),
        P(),
        P(COL, None),
        P(),
        P(),
    )
    return jax.shard_map(
        per_device,
        mesh=grid,
        in_specs=placed,
        out_specs=(P(SEG, None), P(SEG, COL, None)),
        check_vma=False,
    )
```

```python
import functools

import jax
import jax.numpy as jnp
from jax import lax
from jax.experimental import pallas as pl
from jax.experimental.pallas import tpu as pltpu
from jax.sharding import Mesh
from jax.sharding import PartitionSpec as P

MESH = pl.DeviceIdType.MESH
F32 = jnp.float32
BF16 = jnp.bfloat16
SEG = ("y", "z")
COL = ("x", "c")
N = 384
NOBS = 1024
W = 48
CR = 24
PER_CLASS = 36
STRAIGHT1 = (3,)
STRAIGHT3 = (0, 1, 2, 3)


def split(value):
    high = value.astype(BF16)
    low = (value - high.astype(F32)).astype(BF16)
    return high, low


def dot(left, right, transposed):
    dims = (((1,), (1 if transposed else 0,)), ((), ()))
    return lax.dot_general(left, right, dims, preferred_element_type=F32)


def product(left, right_high, right_low, transposed=False):
    high, low = split(left)
    rows = left.shape[0]
    both = dot(jnp.concatenate([high, low], 0), right_high, transposed)
    return both[:rows] + (both[rows:] + dot(high, right_low, transposed))


def put_split(high_ref, low_ref, index, value):
    high, low = split(value)
    high_ref[index] = high
    low_ref[index] = low


def turn(position, by):
    return lax.rem(position + (by % 4), 4)


class PlaneGather:
    def __init__(self, unit, rows, core, first, second, to_first, to_second, partner, send, recv, base, sent, straight, sharing=True):
        self.unit, self.rows, self.core = unit, rows, core
        self.f = [turn(first, d) for d in (0, -1, 1, 2)]
        self.s = [turn(second, d) for d in (0, -1, 1, 2)]
        self.to_first, self.to_second, self.partner = to_first, to_second, partner
        self.send, self.recv, self.base, self.sent, self.straight = send, recv, base, sent, straight
        self.sharing = sharing

    def at(self, kf, ks, half=None, core=None):
        ref = self.unit(self.core if core is None else core, self.f[kf], self.s[ks])
        if half is None:
            return ref
        middle = self.rows // 16 * 8
        return ref.at[pl.ds(0, middle)] if half == 0 else ref.at[pl.ds(middle, self.rows - middle)]

    def start(self, index, source, target, device):
        copy = pltpu.make_async_remote_copy(
            src_ref=source,
            dst_ref=target,
            send_sem=self.send.at[self.base + index],
            recv_sem=self.recv.at[self.base + index],
            device_id=device,
            device_id_type=MESH,
        )
        copy.start()
        self.sent.append(copy)

    def arrive(self, index, slot):
        pltpu.make_async_remote_copy(
            src_ref=slot,
            dst_ref=slot,
            send_sem=self.send.at[self.base + index],
            recv_sem=self.recv.at[self.base + index],
            device_id=self.partner,
            device_id_type=MESH,
        ).wait_recv()

    def first_own(self, source):
        for way in (0, 1):
            self.start(way, source, self.at(0, 0), self.to_first[way])

    def first_own_far(self, source):
        self.start(2, source, self.at(0, 0), self.to_first[2])

    def share(self, kf, ks, source=None):
        if not self.sharing:
            return
        slot = self.at(kf, ks)
        self.start(20 + 4 * ks + kf, slot if source is None else source, slot, self.partner)

    def shared(self, kf, ks):
        self.arrive(20 + 4 * ks + kf, self.at(kf, ks, core=1 - self.core))

    def second(self, kf, source=None):
        slot = self.at(kf, 0)
        source = slot if source is None else source
        for way in (0, 1):
            self.start(4 + 2 * kf + way, source, slot, self.to_second[way])
        if kf in self.straight:
            self.start(12 + 2 * kf, source, slot, self.to_second[2])

    def first_near(self):
        for way in (0, 1):
            self.arrive(way, self.at(1 + way, 0))
            self.second(1 + way)
            self.share(1 + way, 0)

    def first_far(self):
        self.arrive(2, self.at(3, 0))
        self.second(3)
        self.share(3, 0)

    def second_near(self, kf):
        for way in (0, 1):
            self.arrive(4 + 2 * kf + way, self.at(kf, 1 + way))
            if kf not in self.straight:
                part = self.at(kf, 1 + way, half=way)
                self.start(12 + 2 * kf + way, part, part, self.to_second[way])
            self.share(kf, 1 + way)

    def second_far(self, kf):
        if kf in self.straight:
            self.arrive(12 + 2 * kf, self.at(kf, 3))
        else:
            for way in (0, 1):
                self.arrive(12 + 2 * kf + way, self.at(kf, 3, half=way))
        self.share(kf, 3)


def kernel(
    mixing, retention, forcing, observations, model_noise, obs_noise, gain, obs_t, prior_mean, prior_factor,
    means, covariances,
    ga, gb, gx, cg, ea, eb, ret4, forc4, obs4, noise4, ret8, forc16, obs16, noise8, on_v, gain_v, gain_h, gain_l,
    obs_v, pm_v, pf_v, ct_h, ct_l, fix_h, fix_l, p_h, p_l, b_h, b_l, off8, wc, gc, wf, gf, stage,
    near_mean, t1_h, t1_l, n1_h, n1_l, t2_h, t2_l, n2_h, n2_l, w0_s, v1_s, v2_s, xs, nz, ph_f, ph_h, ph_l,
    send1, recv1, send3, recv3, send_c, recv_c, send_g, recv_g, send_s, recv_s, send_y, recv_y, send_m, recv_m, send_b, recv_b, local,
):
    y, z, x, c = (lax.axis_index(name) for name in ("y", "z", "x", "c"))
    partner = (y, z, x, 1 - c)
    x_to = [(y, z, turn(x, d), c) for d in (1, -1, 2)]
    z_to = [(y, turn(z, d), x, c) for d in (1, -1, 2)]
    y_to = [(turn(y, d), z, x, c) for d in (1, 2, 3)]
    sent = []

    own = {}
    for index, (name, source, target) in enumerate(
        (
            ("gain", gain, gain_v),
            ("obs_t", obs_t, obs_v),
            ("mix0", mixing.at[0], ga.at[c, z, x]),
            ("mix1", mixing.at[1], gb.at[c, x, z]),
            ("noise", obs_noise, on_v),
            ("ret", retention, ret4.at[z]),
            ("forc", forcing, forc4.at[z]),
            ("obs", observations, obs4.at[z]),
            ("mn", model_noise, noise4.at[z]),
            ("pm", prior_mean, pm_v),
            ("pf", prior_factor, pf_v),
        )
    ):
        own[name] = pltpu.make_async_copy(source, target, local.at[index])
        own[name].start()

    ea[c, z, x] = jnp.zeros((CR, N), F32)
    eb[c, x, z] = jnp.zeros((CR, N), F32)
    forc16[...] = jnp.zeros((16, N), F32)
    obs16[...] = jnp.zeros((16, NOBS), F32)

    barrier = pltpu.get_barrier_semaphore()
    friends = [partner] + x_to + z_to + y_to
    for friend in friends:
        pl.semaphore_signal(barrier, inc=1, device_id=friend, device_id_type=MESH)

    own["gain"].wait()
    own["obs_t"].wait()
    own["noise"].wait()
    put_split(gain_h, gain_l, ..., gain_v[...])
    rows_of = lax.broadcasted_iota(jnp.int32, (W, N), 0)
    cols_of = lax.broadcasted_iota(jnp.int32, (W, N), 1)
    start_row = x * 96 + c * W
    eye_rows = (rows_of + start_row == cols_of).astype(F32)
    cg[c, x] = eye_rows - product(obs_v[...], gain_h[...], gain_l[...], True)
    for part in range(3):
        rows = pl.ds(part * 128, 128)
        put_split(fix_h, fix_l, rows, product(gain_v[rows, :] * on_v[...], gain_h[...], gain_l[...], True))

    own["pf"].wait()

    @pl.when(y == 0)
    def _():
        high, low = split(pf_v[...])
        put_split(p_h, p_l, ..., product(pf_v[...], high, low, True))

    pl.semaphore_wait(barrier, len(friends))

    first = PlaneGather(lambda core, f, s: ga.at[core, s, f], W, c, x, z, x_to, z_to, partner, send1, recv1, 0, sent, STRAIGHT1, False)
    other = PlaneGather(
        lambda core, f, s: gb.at[core, s, f], W, c, z, x, z_to, x_to, partner, send1, recv1, PER_CLASS, sent, STRAIGHT1, False
    )

    def gain_copy(index, slot, device):
        return pltpu.make_async_remote_copy(
            src_ref=slot,
            dst_ref=slot,
            send_sem=send_c.at[index],
            recv_sem=recv_c.at[index],
            device_id=device,
            device_id_type=MESH,
        )

    def third_of(place, part):
        return cg.at[c, place, pl.ds(16 * part, 16)]

    @pl.when(y < 3)
    def _():
        for index, device in enumerate(x_to):
            gain_copy(index, third_of(x, y), device).start()

    for gather, step in ((first, 0), (other, 1)):
        gather.first_own(mixing.at[step])
    for gather, step in ((first, 0), (other, 1)):
        gather.first_own_far(mixing.at[step])
    for gather, step in ((first, 0), (other, 1)):
        gather.second(0, mixing.at[step])
    gain_copy(3, cg.at[c, x], partner).start()
    for gather, step in ((first, 0), (other, 1)):
        gather.share(0, 0, mixing.at[step])

    small = []
    for array, (source, target) in enumerate(
        ((retention, ret4), (forcing, forc4), (observations, obs4), (model_noise, noise4))
    ):
        for d in (1, 2, 3):
            index = 3 * array + d - 1
            copy = pltpu.make_async_remote_copy(
                src_ref=source,
                dst_ref=target.at[z],
                send_sem=send_s.at[index],
                recv_sem=recv_s.at[index],
                device_id=(y, turn(z, d), x, c),
                device_id_type=MESH,
            )
            copy.start()
            sent.append(copy)
            slot = target.at[turn(z, -d)]
            small.append(
                pltpu.make_async_remote_copy(
                    src_ref=slot,
                    dst_ref=slot,
                    send_sem=send_s.at[index],
                    recv_sem=recv_s.at[index],
                    device_id=partner,
                    device_id_type=MESH,
                )
            )


    @pl.when(y < 3)
    def _():
        for index, d in enumerate((-1, 1, 2)):
            slot = third_of(turn(x, d), y)
            gain_copy(index, slot, partner).wait_recv()
            for way in range(3):
                copy = pltpu.make_async_remote_copy(
                    src_ref=slot,
                    dst_ref=slot,
                    send_sem=send_g.at[3 * way + index],
                    recv_sem=recv_g.at[3 * y + index],
                    device_id=y_to[way],
                    device_id_type=MESH,
                )
                copy.start()

    def drain():
        for copy in sent:
            copy.wait_send()
        for index in range(8):
            swap(index, c).wait_send()
        swap_phi(c).wait_send()

        @pl.when(c == 0)
        def _():
            ships(True, lambda copy: copy.wait_send())

        @pl.when(c == 1)
        def _():
            ships(False, lambda copy: copy.wait_send())
            for plane in range(3):

                @pl.when(y > plane)
                def _():
                    pass_mean(plane).wait_send()

        @pl.when(y < 3)
        def _():
            for index, device in enumerate(x_to):
                gain_copy(index, third_of(x, y), device).wait_send()
            for index, d in enumerate((-1, 1, 2)):
                slot = third_of(turn(x, d), y)
                for way in range(3):
                    pltpu.make_async_remote_copy(
                        src_ref=slot,
                        dst_ref=slot,
                        send_sem=send_g.at[3 * way + index],
                        recv_sem=recv_g.at[3 * y + index],
                        device_id=y_to[way],
                        device_id_type=MESH,
                    ).wait_send()

        for index in range(3):
            gain_copy(4 + index, cg.at[c, x], partner).wait_send()
        gain_copy(3, cg.at[c, x], partner).wait_send()

    first.first_near()
    other.first_near()
    first.first_far()
    other.first_far()
    first.second_near(0)
    other.second_near(0)
    for part in range(3):

        @pl.when(y != part)
        def _():
            for index, d in enumerate((-1, 1, 2)):
                slot = third_of(turn(x, d), part)
                pltpu.make_async_remote_copy(
                    src_ref=slot,
                    dst_ref=slot,
                    send_sem=send_g.at[0],
                    recv_sem=recv_g.at[3 * part + index],
                    device_id=partner,
                    device_id_type=MESH,
                ).wait_recv()

    for index, d in enumerate((-1, 1, 2)):
        gain_copy(4 + index, cg.at[c, turn(x, d)], partner).start()

    for name in ("ret", "forc", "obs", "mn", "pm", "mix0", "mix1"):
        own[name].wait()
    for copy in small:
        copy.wait_recv()
    for place in range(4):
        for step in range(2):
            row = 2 * place + step
            ret8[pl.ds(row, 1), :] = ret4[place, pl.ds(step, 1), :]
            noise8[pl.ds(row, 1), :] = noise4[place, pl.ds(step, 1), :]
            forc16[pl.ds(row, 1), :] = forc4[place, pl.ds(step, 1), :]
            obs16[pl.ds(row, 1), :] = obs4[place, pl.ds(step, 1), :]

    gain_copy(3, cg.at[1 - c, x], partner).wait_recv()
    for index, d in enumerate((-1, 1, 2)):
        gain_copy(4 + index, cg.at[1 - c, turn(x, d)], partner).wait_recv()
    put_split(ct_h, ct_l, ..., jnp.concatenate([cg[core, place] for place in range(4) for core in range(2)], 0))
    offsets = product(forc16[...], ct_h[...], ct_l[...]) + product(obs16[...], gain_h[...], gain_l[...], True)
    off8[...] = offsets[:8]

    def swap(index, core):
        slot = gx.at[core, index]
        return pltpu.make_async_remote_copy(
            src_ref=slot,
            dst_ref=slot,
            send_sem=send_b.at[index],
            recv_sem=recv_b.at[index],
            device_id=partner,
            device_id_type=MESH,
        )

    def put_first(ks, core, value):
        high, low = split(value)
        for spot in range(4):
            target = pl.ds(pl.multiple_of(spot * 96 + core * W, 16), W)
            b_h[2 * first.s[ks], target, :] = high[W * spot : W * (spot + 1)]
            b_l[2 * first.s[ks], target, :] = low[W * spot : W * (spot + 1)]

    def put_other(ks, core, value):
        high, low = split(value)
        target = pl.ds(pl.multiple_of(other.s[ks] * 96 + core * W, 16), W)
        for spot in range(4):
            b_h[2 * spot + 1, target, :] = high[W * spot : W * (spot + 1)]
            b_l[2 * spot + 1, target, :] = low[W * spot : W * (spot + 1)]

    def kept(row, offset):
        return jnp.where(rows_of + offset == cols_of, ret8[pl.ds(row, 1), :], 0.0)

    def step_first(ks):
        place = first.s[ks]
        raw = [ga[c, place, spot] + kept(2 * place, spot * 96 + c * W) for spot in range(4)]
        value = product(jnp.concatenate(raw, 0), ct_h[...], ct_l[...])
        gx[c, ks] = value
        put_first(ks, c, value)
        swap(ks, c).start()

    def step_other(ks):
        place = other.s[ks]
        raw = [gb[c, place, spot] + kept(2 * spot + 1, place * 96 + c * W) for spot in range(4)]
        value = product(jnp.concatenate(raw, 0), ct_h[...], ct_l[...])
        gx[c, 4 + ks] = value
        put_other(ks, c, value)
        swap(4 + ks, c).start()

    def take_first(ks):
        swap(ks, 1 - c).wait_recv()
        put_first(ks, 1 - c, gx[1 - c, ks])

    def take_other(ks):
        swap(4 + ks, 1 - c).wait_recv()
        put_other(ks, 1 - c, gx[1 - c, 4 + ks])

    def ready(gather, ks):
        for kf in range(4):
            gather.shared(kf, ks)

    step_first(0)
    first.second_near(1)
    other.second_near(1)
    step_other(0)
    first.second_near(2)
    other.second_near(2)
    take_first(0)
    first.second_near(3)
    other.second_near(3)
    step_first(1)
    first.second_far(0)
    other.second_far(0)
    step_first(2)
    first.second_far(1)
    other.second_far(1)
    step_other(1)
    first.second_far(2)
    other.second_far(2)
    step_other(2)
    take_other(0)
    take_first(1)
    take_first(2)
    take_other(1)
    first.second_far(3)
    other.second_far(3)
    step_first(3)
    step_other(3)
    take_other(2)
    take_first(3)
    take_other(3)

    row32 = lax.broadcasted_iota(jnp.int32, (32, N), 0)
    col32 = lax.broadcasted_iota(jnp.int32, (32, N), 1)
    start24 = (z * 4 + x) * CR
    walk = ((row32 < CR) & (row32 + start24 == col32)).astype(F32)
    for j in range(7, -1, -1):
        wc[j] = walk
        walk = product(walk, b_h[j], b_l[j], True)
    stage[1] = walk
    mine_a, mine_b = ea.at[c, z, x], eb.at[c, x, z]

    def ship(index, source, target, slot, device):
        return pltpu.make_async_remote_copy(
            src_ref=source,
            dst_ref=target,
            send_sem=send_y.at[index],
            recv_sem=recv_y.at[slot],
            device_id=device,
            device_id_type=MESH,
        )

    def ships(first_core, act):
        near, far = pl.ds(0, 256), pl.ds(256, 128)
        if first_core:

            @pl.when(y == 1)
            def _():
                for d in range(2):
                    act(ship(d, stage.at[1, pl.ds(0, CR)], mine_a, 2, y_to[d]))

            @pl.when(y == 2)
            def _():
                act(ship(0, stage.at[1, pl.ds(0, CR)], mine_b, 3, y_to[0]))

            return
        packed, mean = stage.at[2, pl.ds(0, CR)], stage.at[0, pl.ds(CR, 8)]

        @pl.when(y == 0)
        def _():
            for d in range(3):
                act(ship(3 * d, packed.at[:, pl.ds(0, 128)], mine_a.at[:, far], 0, y_to[d]))
                act(ship(3 * d + 1, packed.at[:, pl.ds(128, 128)], mine_b.at[:, far], 1, y_to[d]))
                act(ship(3 * d + 2, mean, near_mean.at[0], 4, y_to[d]))

        @pl.when(y == 1)
        def _():
            for d in range(2):
                act(ship(2 * d, packed.at[:, near], mine_a.at[:, near], 2, y_to[d]))
                act(ship(2 * d + 1, mean, near_mean.at[1], 5, y_to[d]))

        @pl.when(y == 2)
        def _():
            act(ship(0, packed.at[:, near], mine_b.at[:, near], 3, y_to[0]))
            act(ship(1, mean, near_mean.at[2], 6, y_to[0]))

    def pass_mean(index):
        return pltpu.make_async_remote_copy(
            src_ref=near_mean.at[index],
            dst_ref=near_mean.at[index],
            send_sem=send_m.at[index],
            recv_sem=recv_m.at[index],
            device_id=partner,
            device_id_type=MESH,
        )

    @pl.when(c == 0)
    def _():
        ships(True, lambda copy: copy.start())

    @pl.when(c == 1)
    def _():
        left = wc[...].reshape(256, N)
        spread = product(left, ct_h[...], ct_l[...], True).reshape(8, 32, N) * noise8[...].reshape(8, 1, N)
        noise = product(spread.reshape(256, N), ct_h[...], ct_l[...]) + product(left, fix_h[...], fix_l[...])
        gc[...] = noise.reshape(8, 32, N)

        @pl.when(y == 0)
        def _():
            begin = product(stage[1], p_h[...], p_l[...])
            stage[0] = jnp.where(row32 == CR, pm_v[...].reshape(1, N), begin)

        @pl.when(y != 0)
        def _():
            stage[0] = jnp.zeros((32, N), F32)

        grown = stage[0]
        for j in range(8):
            grown = product(grown, b_h[j], b_l[j])
            grown = grown + gc[j] + jnp.where(row32 == CR, off8[pl.ds(j, 1), :], 0.0)
        stage[0] = grown
        band = row32[:, :128] + start24
        low, high = band < 128, band >= 256
        one, two, three = (grown[:, 128 * b : 128 * (b + 1)] for b in range(3))
        stage[2, :, pl.ds(0, 128)] = jnp.where(low, one, jnp.where(high, three, two))
        stage[2, :, pl.ds(128, 128)] = jnp.where(low, two, jnp.where(high, one, three))
        ships(False, lambda copy: copy.start())

    last = 2 * z + 1
    wf[last, pl.ds(W, W), :] = eye_rows
    behind = product(eye_rows, b_h[last], b_l[last], True)
    w0_s[pl.ds(0, W), :] = eye_rows
    w0_s[pl.ds(W, W), :] = behind

    @pl.loop(0, 2 * z + 1)
    def _(i):
        j = 2 * z - i
        rows = w0_s[...]
        wf[j] = rows
        w0_s[...] = product(rows, b_h[j], b_l[j], True)

    def noise_rows(part):
        span = pl.ds(4 * part, 4)
        rows = wf[span].reshape(N, N)
        wide = product(rows, ct_h[...], ct_l[...], True).reshape(4, 96, N)
        wide = wide * noise8[pl.ds(4 * part, 4), :].reshape(4, 1, N)
        value = product(wide.reshape(N, N), ct_h[...], ct_l[...]) + product(rows, fix_h[...], fix_l[...])
        gf[span] = value.reshape(4, 96, N)


    @pl.when((c == 0) & (y >= 2))
    def _():
        ship(0, mine_a, mine_a, 2, partner).wait_recv()

    @pl.when((c == 0) & (y >= 3))
    def _():
        ship(0, mine_b, mine_b, 3, partner).wait_recv()

    @pl.when((c == 1) & (y >= 1))
    def _():
        ship(0, mine_a.at[:, pl.ds(256, 128)], mine_a.at[:, pl.ds(256, 128)], 0, partner).wait_recv()
        ship(0, mine_b.at[:, pl.ds(256, 128)], mine_b.at[:, pl.ds(256, 128)], 1, partner).wait_recv()

    @pl.when((c == 1) & (y >= 2))
    def _():
        ship(0, mine_a.at[:, pl.ds(0, 256)], mine_a.at[:, pl.ds(0, 256)], 2, partner).wait_recv()

    @pl.when((c == 1) & (y >= 3))
    def _():
        ship(0, mine_b.at[:, pl.ds(0, 256)], mine_b.at[:, pl.ds(0, 256)], 3, partner).wait_recv()

    third = PlaneGather(lambda core, f, s: ea.at[core, s, f], CR, c, x, z, x_to, z_to, partner, send3, recv3, 0, sent, STRAIGHT3)
    fourth = PlaneGather(
        lambda core, f, s: eb.at[core, s, f], CR, c, z, x, z_to, x_to, partner, send3, recv3, PER_CLASS, sent, STRAIGHT3
    )
    for gather in (third, fourth):
        gather.first_own(gather.at(0, 0))
    for gather in (third, fourth):
        gather.first_own_far(gather.at(0, 0))
    for gather in (third, fourth):
        gather.second(0)
        gather.share(0, 0)

    for plane in range(3):

        @pl.when((c == 1) & (y > plane))
        def _():
            ship(0, near_mean.at[plane], near_mean.at[plane], 4 + plane, partner).wait_recv()
            pass_mean(plane).start()

    own_half = pl.ds(pl.multiple_of(c * 192, 64), 192)
    ph_f[c] = b_h[0, own_half, :].astype(F32) + b_l[0, own_half, :].astype(F32)

    @pl.loop(1, 2 * z + 1)
    def _(j):
        ph_f[c] = product(ph_f[c], b_h[j], b_l[j])

    def swap_phi(core):
        slot = ph_f.at[core]
        return pltpu.make_async_remote_copy(
            src_ref=slot,
            dst_ref=slot,
            send_sem=send_b.at[8],
            recv_sem=recv_b.at[8],
            device_id=partner,
            device_id_type=MESH,
        )

    third.first_near()
    fourth.first_near()
    third.first_far()
    fourth.first_far()
    swap_phi(c).start()
    noise_rows(0)

    third.second_near(0)
    fourth.second_near(0)

    @pl.when(z >= 2)
    def _():
        noise_rows(1)

    for kf in (1, 2):
        third.second_near(kf)
        fourth.second_near(kf)

    row16 = lax.broadcasted_iota(jnp.int32, (16, N), 0)

    def mean_rows(row):
        return jnp.where(row16 == 0, row, 0.0)

    def fresh(j):
        return jnp.concatenate([gf[j], mean_rows(off8[pl.ds(j, 1), :])], 0)

    nz[...] = fresh(0)

    @pl.loop(1, z + 1)
    def _(j):
        nz[...] = product(nz[...], b_h[j], b_l[j]) + fresh(j)

    third.second_near(3)
    fourth.second_near(3)

    @pl.loop(z + 1, 2 * z + 1)
    def _(j):
        nz[...] = product(nz[...], b_h[j], b_l[j]) + fresh(j)

    swap_phi(1 - c).wait_recv()
    for core in range(2):
        high, low = split(ph_f[core])
        ph_h[pl.ds(192 * core, 192), :] = high
        ph_l[pl.ds(192 * core, 192), :] = low

    spots = [(a, b) for a in range(4) for b in range(4)]

    def symmetric(own, after):
        d0, d1, d2 = (own[128 * b : 128 * (b + 1)] for b in range(3))
        u0, u1, u2 = (after[128 * b : 128 * (b + 1)] for b in range(3))
        rows = ((d0, u0, u2.T), (u0.T, d1, u1), (u2, u1.T, d2))
        return jnp.concatenate([jnp.concatenate(row, 1) for row in rows], 0)

    def columns(pick, block):
        return jnp.concatenate([pick(a, b)[:, 128 * block : 128 * (block + 1)] for a, b in spots], 0)

    def from_a(a, b):
        return ea[1, a, b]

    def from_b(a, b):
        return eb[1, b, a]

    def ready_all():
        for ks in range(4):
            ready(third, ks)
            ready(fourth, ks)

    def prepare_steps():
        @pl.when(y == 3)
        def _():
            put_split(t2_h, t2_l, ..., jnp.concatenate([eb[0, b, a] for a, b in spots], 0))
            v2_s[...] = product(w0_s[...], t2_h[...], t2_l[...])

        @pl.when(y != 3)
        def _():
            v2_s[...] = w0_s[...]

        @pl.when(y >= 2)
        def _():
            put_split(t1_h, t1_l, ..., jnp.concatenate([ea[0, a, b] for a, b in spots], 0))
            v1_s[...] = product(v2_s[...], t1_h[...], t1_l[...])

        @pl.when(y < 2)
        def _():
            v1_s[...] = v2_s[...]

    for kf in range(4):
        third.second_far(kf)
        fourth.second_far(kf)

    @pl.when(c == 0)
    def _():
        prepare_steps()
        ready_all()

    @pl.when(c == 1)
    def _():
        ready_all()
        prepare_steps()

    for plane in range(3):

        @pl.when((c == 0) & (y > plane))
        def _():
            pass_mean(plane).wait_recv()

    def covariance_before():
        return split(symmetric(columns(from_a, 2), columns(from_b, 2)))

    def mean_of(plane):
        return mean_rows(near_mean[plane, pl.ds(0, 1), :])

    def joined(rows, row):
        return jnp.concatenate([rows, row], 0)

    @pl.when(y == 0)
    def _():
        xs[...] = joined(product(v1_s[...], p_h[...], p_l[...]), mean_rows(pm_v[...].reshape(1, N)))

    @pl.when(y == 1)
    def _():
        xs[...] = joined(product(v1_s[...], *covariance_before()), mean_of(0))

    @pl.when(y >= 2)
    def _():
        value = joined(product(v1_s[...], *covariance_before()), mean_of(0))
        added = product(v2_s[...], *split(symmetric(columns(from_a, 0), columns(from_a, 1))))
        xs[...] = product(value, t1_h[...], t1_l[...], True) + joined(added, mean_of(1))

    @pl.when(y >= 3)
    def _():
        added = product(w0_s[...], *split(symmetric(columns(from_b, 0), columns(from_b, 1))))
        xs[...] = product(xs[...], t2_h[...], t2_l[...], True) + joined(added, mean_of(2))

    xs[...] = product(xs[...], ph_h[...], ph_l[...]) + nz[...]

    covariances[0] = xs[pl.ds(0, W), :]
    means[pl.ds(0, 1), :] = xs[pl.ds(96, 1), :]
    value = product(xs[pl.ds(W, 64), :], b_h[last], b_l[last])
    covariances[1] = value[:W] + gf[last, pl.ds(W, W), :]
    means[pl.ds(1, 1), :] = value[W : W + 1] + off8[pl.ds(last, 1), :]
    drain()


def finish(near_means, near_covariances, means, covariances, done):
    copies = [
        pltpu.make_async_copy(near_means, means, done.at[0]),
        pltpu.make_async_copy(near_covariances, covariances, done.at[1]),
    ]
    for copy in copies:
        copy.start()
    for copy in copies:
        copy.wait()


def vmem(shape, dtype=F32):
    return pltpu.VMEM(shape, dtype)


def pair(shape):
    return [vmem(shape, BF16), vmem(shape, BF16)]


def per_device(mixing, retention, forcing, observations, model_noise, obs_noise, gain, obs_t, prior_mean, prior_factor):
    dma = pltpu.SemaphoreType.DMA
    square = (N, N)
    near = pl.pallas_call(
        kernel,
        out_shape=(pltpu.VMEM((2, N), F32), pltpu.VMEM((2, W, N), F32)),
        in_specs=[pl.BlockSpec(memory_space=pltpu.HBM)] * 10,
        out_specs=(pl.BlockSpec(memory_space=pltpu.VMEM),) * 2,
        scratch_shapes=[
            vmem((2, 4, 4, W, N)),
            vmem((2, 4, 4, W, N)),
            vmem((2, 8, 4 * W, N)),
            vmem((2, 4, W, N)),
            vmem((2, 4, 4, CR, N)),
            vmem((2, 4, 4, CR, N)),
            vmem((4, 2, N)),
            vmem((4, 2, N)),
            vmem((4, 2, NOBS)),
            vmem((4, 2, N)),
            vmem((8, N)),
            vmem((16, N)),
            vmem((16, NOBS)),
            vmem((8, N)),
            vmem((1, NOBS)),
            vmem((N, NOBS)),
            *pair((N, NOBS)),
            vmem((W, NOBS)),
            vmem((N,)),
            vmem(square),
            *pair(square),
            *pair(square),
            *pair(square),
            *pair((8, N, N)),
            vmem((8, N)),
            vmem((8, 32, N)),
            vmem((8, 32, N)),
            vmem((8, 96, N)),
            vmem((8, 96, N)),
            vmem((3, 32, N)),
            vmem((3, 8, N)),
            *pair(square),
            *pair(square),
            *pair(square),
            *pair(square),
            vmem((96, N)),
            vmem((96, N)),
            vmem((96, N)),
            vmem((112, N)),
            vmem((112, N)),
            vmem((2, 192, N)),
            *pair(square),
            dma((2 * PER_CLASS,)),
            dma((2 * PER_CLASS,)),
            dma((2 * PER_CLASS,)),
            dma((2 * PER_CLASS,)),
            dma((7,)),
            dma((7,)),
            dma((9,)),
            dma((9,)),
            dma((12,)),
            dma((12,)),
            dma((9,)),
            dma((7,)),
            dma((3,)),
            dma((3,)),
            dma((9,)),
            dma((9,)),
            dma((11,)),
        ],
        compiler_params=pltpu.CompilerParams(
            collective_id=0, has_side_effects=True, vmem_limit_bytes=60 * 1024 * 1024
        ),
        name="prefix",
    )(
        mixing, retention, forcing, observations, model_noise, obs_noise.reshape(1, NOBS), gain, obs_t,
        prior_mean, prior_factor,
    )
    return pl.pallas_call(
        finish,
        out_shape=(jax.ShapeDtypeStruct((2, N), F32), jax.ShapeDtypeStruct((2, W, N), F32)),
        in_specs=[pl.BlockSpec(memory_space=pltpu.VMEM)] * 2,
        out_specs=(pl.BlockSpec(memory_space=pltpu.HBM),) * 2,
        scratch_shapes=[pltpu.SemaphoreType.DMA((2,))],
        compiler_params=pltpu.CompilerParams(vmem_limit_bytes=1024 * 1024),
        name="finish",
    )(*near)


def solution(mesh):
    grid = Mesh(mesh.devices.reshape(4, 4, 4, 2), SEG + COL)
    placed = (
        P(SEG, COL, None),
        P(SEG, None),
        P(SEG, None),
        P(SEG, None),
        P(SEG, None),
        P(),
        P(),
        P(COL, None),
        P(),
        P(),
    )
    return jax.shard_map(
        per_device,
        mesh=grid,
        in_specs=placed,
        out_specs=(P(SEG, None), P(SEG, COL, None)),
        check_vma=False,
    )
```

```python
import functools

import jax
import jax.numpy as jnp
from jax import lax
from jax.experimental import pallas as pl
from jax.experimental.pallas import tpu as pltpu
from jax.sharding import Mesh
from jax.sharding import PartitionSpec as P

MESH = pl.DeviceIdType.MESH
F32 = jnp.float32
BF16 = jnp.bfloat16
SEG = ("y", "z")
COL = ("x", "c")
N = 384
NOBS = 1024
W = 48
CR = 24
PER_CLASS = 36
STRAIGHT1 = (3,)
STRAIGHT3 = (0, 1, 2, 3)


def split(value):
    high = value.astype(BF16)
    low = (value - high.astype(F32)).astype(BF16)
    return high, low


def dot(left, right, transposed):
    dims = (((1,), (1 if transposed else 0,)), ((), ()))
    return lax.dot_general(left, right, dims, preferred_element_type=F32)


def product(left, right_high, right_low, transposed=False):
    high, low = split(left)
    rows = left.shape[0]
    both = dot(jnp.concatenate([high, low], 0), right_high, transposed)
    return both[:rows] + (both[rows:] + dot(high, right_low, transposed))


def put_split(high_ref, low_ref, index, value):
    high, low = split(value)
    high_ref[index] = high
    low_ref[index] = low


def turn(position, by):
    return lax.rem(position + (by % 4), 4)


class PlaneGather:
    def __init__(self, unit, rows, core, first, second, to_first, to_second, partner, send, recv, base, sent, straight, sharing=True):
        self.unit, self.rows, self.core = unit, rows, core
        self.f = [turn(first, d) for d in (0, -1, 1, 2)]
        self.s = [turn(second, d) for d in (0, -1, 1, 2)]
        self.to_first, self.to_second, self.partner = to_first, to_second, partner
        self.send, self.recv, self.base, self.sent, self.straight = send, recv, base, sent, straight
        self.sharing = sharing

    def at(self, kf, ks, half=None, core=None):
        ref = self.unit(self.core if core is None else core, self.f[kf], self.s[ks])
        if half is None:
            return ref
        middle = self.rows // 16 * 8
        return ref.at[pl.ds(0, middle)] if half == 0 else ref.at[pl.ds(middle, self.rows - middle)]

    def start(self, index, source, target, device):
        copy = pltpu.make_async_remote_copy(
            src_ref=source,
            dst_ref=target,
            send_sem=self.send.at[self.base + index],
            recv_sem=self.recv.at[self.base + index],
            device_id=device,
            device_id_type=MESH,
        )
        copy.start()
        self.sent.append(copy)

    def arrive(self, index, slot):
        pltpu.make_async_remote_copy(
            src_ref=slot,
            dst_ref=slot,
            send_sem=self.send.at[self.base + index],
            recv_sem=self.recv.at[self.base + index],
            device_id=self.partner,
            device_id_type=MESH,
        ).wait_recv()

    def first_own(self, source):
        for way in (0, 1):
            self.start(way, source, self.at(0, 0), self.to_first[way])

    def first_own_far(self, source):
        self.start(2, source, self.at(0, 0), self.to_first[2])

    def share(self, kf, ks, source=None):
        if not self.sharing:
            return
        slot = self.at(kf, ks)
        self.start(20 + 4 * ks + kf, slot if source is None else source, slot, self.partner)

    def shared(self, kf, ks):
        self.arrive(20 + 4 * ks + kf, self.at(kf, ks, core=1 - self.core))

    def second(self, kf, source=None):
        slot = self.at(kf, 0)
        source = slot if source is None else source
        for way in (0, 1):
            self.start(4 + 2 * kf + way, source, slot, self.to_second[way])
        if kf in self.straight:
            self.start(12 + 2 * kf, source, slot, self.to_second[2])

    def first_near(self):
        for way in (0, 1):
            self.arrive(way, self.at(1 + way, 0))
            self.second(1 + way)
            self.share(1 + way, 0)

    def first_far(self):
        self.arrive(2, self.at(3, 0))
        self.second(3)
        self.share(3, 0)

    def second_near(self, kf):
        for way in (0, 1):
            self.arrive(4 + 2 * kf + way, self.at(kf, 1 + way))
            if kf not in self.straight:
                part = self.at(kf, 1 + way, half=way)
                self.start(12 + 2 * kf + way, part, part, self.to_second[way])
            self.share(kf, 1 + way)

    def second_far(self, kf):
        if kf in self.straight:
            self.arrive(12 + 2 * kf, self.at(kf, 3))
        else:
            for way in (0, 1):
                self.arrive(12 + 2 * kf + way, self.at(kf, 3, half=way))
        self.share(kf, 3)


def kernel(
    mixing, retention, forcing, observations, model_noise, obs_noise, gain, obs_t, prior_mean, prior_factor,
    means, covariances,
    ga, gb, gx, cg, ea, eb, ret4, forc4, obs4, noise4, ret8, forc16, obs16, noise8, on_v, gain_v, gain_h, gain_l,
    obs_v, pm_v, pf_v, ct_h, ct_l, fix_h, fix_l, p_h, p_l, b_h, b_l, off8, wc, gc, wf, gf, stage,
    near_mean, t1_h, t1_l, n1_h, n1_l, t2_h, t2_l, n2_h, n2_l, w0_s, v1_s, v2_s, xs, nz, ph_f, ph_h, ph_l,
    send1, recv1, send3, recv3, send_c, recv_c, send_g, recv_g, send_s, recv_s, send_y, recv_y, send_m, recv_m, send_b, recv_b, local,
):
    y, z, x, c = (lax.axis_index(name) for name in ("y", "z", "x", "c"))
    partner = (y, z, x, 1 - c)
    x_to = [(y, z, turn(x, d), c) for d in (1, -1, 2)]
    z_to = [(y, turn(z, d), x, c) for d in (1, -1, 2)]
    y_to = [(turn(y, d), z, x, c) for d in (1, 2, 3)]
    sent = []

    own = {}
    for index, (name, source, target) in enumerate(
        (
            ("gain", gain, gain_v),
            ("obs_t", obs_t, obs_v),
            ("mix0", mixing.at[0], ga.at[c, z, x]),
            ("mix1", mixing.at[1], gb.at[c, x, z]),
            ("noise", obs_noise, on_v),
            ("ret", retention, ret4.at[z]),
            ("forc", forcing, forc4.at[z]),
            ("obs", observations, obs4.at[z]),
            ("mn", model_noise, noise4.at[z]),
            ("pm", prior_mean, pm_v),
            ("pf", prior_factor, pf_v),
        )
    ):
        own[name] = pltpu.make_async_copy(source, target, local.at[index])
        own[name].start()

    ea[c, z, x] = jnp.zeros((CR, N), F32)
    eb[c, x, z] = jnp.zeros((CR, N), F32)
    forc16[...] = jnp.zeros((16, N), F32)
    obs16[...] = jnp.zeros((16, NOBS), F32)

    barrier = pltpu.get_barrier_semaphore()
    friends = [partner] + x_to + z_to + y_to
    for friend in friends:
        pl.semaphore_signal(barrier, inc=1, device_id=friend, device_id_type=MESH)

    own["gain"].wait()
    own["obs_t"].wait()
    own["noise"].wait()
    put_split(gain_h, gain_l, ..., gain_v[...])
    rows_of = lax.broadcasted_iota(jnp.int32, (W, N), 0)
    cols_of = lax.broadcasted_iota(jnp.int32, (W, N), 1)
    start_row = x * 96 + c * W
    eye_rows = (rows_of + start_row == cols_of).astype(F32)
    cg[c, x] = eye_rows - product(obs_v[...], gain_h[...], gain_l[...], True)
    for part in range(3):
        rows = pl.ds(part * 128, 128)
        put_split(fix_h, fix_l, rows, product(gain_v[rows, :] * on_v[...], gain_h[...], gain_l[...], True))

    own["pf"].wait()

    @pl.when(y == 0)
    def _():
        high, low = split(pf_v[...])
        put_split(p_h, p_l, ..., product(pf_v[...], high, low, True))

    pl.semaphore_wait(barrier, len(friends))

    first = PlaneGather(lambda core, f, s: ga.at[core, s, f], W, c, x, z, x_to, z_to, partner, send1, recv1, 0, sent, STRAIGHT1, False)
    other = PlaneGather(
        lambda core, f, s: gb.at[core, s, f], W, c, z, x, z_to, x_to, partner, send1, recv1, PER_CLASS, sent, STRAIGHT1, False
    )

    def gain_copy(index, slot, device):
        return pltpu.make_async_remote_copy(
            src_ref=slot,
            dst_ref=slot,
            send_sem=send_c.at[index],
            recv_sem=recv_c.at[index],
            device_id=device,
            device_id_type=MESH,
        )

    def third_of(place, part):
        return cg.at[c, place, pl.ds(16 * part, 16)]

    @pl.when(y < 3)
    def _():
        for index, device in enumerate(x_to):
            gain_copy(index, third_of(x, y), device).start()

    for gather, step in ((first, 0), (other, 1)):
        gather.first_own(mixing.at[step])
    for gather, step in ((first, 0), (other, 1)):
        gather.first_own_far(mixing.at[step])
    for gather, step in ((first, 0), (other, 1)):
        gather.second(0, mixing.at[step])
    gain_copy(3, cg.at[c, x], partner).start()
    for gather, step in ((first, 0), (other, 1)):
        gather.share(0, 0, mixing.at[step])

    small = []
    for array, (source, target) in enumerate(
        ((retention, ret4), (forcing, forc4), (observations, obs4), (model_noise, noise4))
    ):
        for d in (1, 2, 3):
            index = 3 * array + d - 1
            copy = pltpu.make_async_remote_copy(
                src_ref=source,
                dst_ref=target.at[z],
                send_sem=send_s.at[index],
                recv_sem=recv_s.at[index],
                device_id=(y, turn(z, d), x, c),
                device_id_type=MESH,
            )
            copy.start()
            sent.append(copy)
            slot = target.at[turn(z, -d)]
            small.append(
                pltpu.make_async_remote_copy(
                    src_ref=slot,
                    dst_ref=slot,
                    send_sem=send_s.at[index],
                    recv_sem=recv_s.at[index],
                    device_id=partner,
                    device_id_type=MESH,
                )
            )


    @pl.when(y < 3)
    def _():
        for index, d in enumerate((-1, 1, 2)):
            slot = third_of(turn(x, d), y)
            gain_copy(index, slot, partner).wait_recv()
            for way in range(3):
                copy = pltpu.make_async_remote_copy(
                    src_ref=slot,
                    dst_ref=slot,
                    send_sem=send_g.at[3 * way + index],
                    recv_sem=recv_g.at[3 * y + index],
                    device_id=y_to[way],
                    device_id_type=MESH,
                )
                copy.start()

    def drain():
        for copy in sent:
            copy.wait_send()
        for index in range(8):
            swap(index, c).wait_send()
        swap_phi(c).wait_send()

        @pl.when(c == 0)
        def _():
            ships(True, lambda copy: copy.wait_send())

        @pl.when(c == 1)
        def _():
            ships(False, lambda copy: copy.wait_send())
            for plane in range(3):

                @pl.when(y > plane)
                def _():
                    pass_mean(plane).wait_send()

        @pl.when(y < 3)
        def _():
            for index, device in enumerate(x_to):
                gain_copy(index, third_of(x, y), device).wait_send()
            for index, d in enumerate((-1, 1, 2)):
                slot = third_of(turn(x, d), y)
                for way in range(3):
                    pltpu.make_async_remote_copy(
                        src_ref=slot,
                        dst_ref=slot,
                        send_sem=send_g.at[3 * way + index],
                        recv_sem=recv_g.at[3 * y + index],
                        device_id=y_to[way],
                        device_id_type=MESH,
                    ).wait_send()

        for index in range(3):
            gain_copy(4 + index, cg.at[c, x], partner).wait_send()
        gain_copy(3, cg.at[c, x], partner).wait_send()

    first.first_near()
    other.first_near()
    first.first_far()
    other.first_far()
    first.second_near(0)
    other.second_near(0)
    for part in range(3):

        @pl.when(y != part)
        def _():
            for index, d in enumerate((-1, 1, 2)):
                slot = third_of(turn(x, d), part)
                pltpu.make_async_remote_copy(
                    src_ref=slot,
                    dst_ref=slot,
                    send_sem=send_g.at[0],
                    recv_sem=recv_g.at[3 * part + index],
                    device_id=partner,
                    device_id_type=MESH,
                ).wait_recv()

    for index, d in enumerate((-1, 1, 2)):
        gain_copy(4 + index, cg.at[c, turn(x, d)], partner).start()

    for name in ("ret", "forc", "obs", "mn", "pm", "mix0", "mix1"):
        own[name].wait()
    for copy in small:
        copy.wait_recv()
    for place in range(4):
        for step in range(2):
            row = 2 * place + step
            ret8[pl.ds(row, 1), :] = ret4[place, pl.ds(step, 1), :]
            noise8[pl.ds(row, 1), :] = noise4[place, pl.ds(step, 1), :]
            forc16[pl.ds(row, 1), :] = forc4[place, pl.ds(step, 1), :]
            obs16[pl.ds(row, 1), :] = obs4[place, pl.ds(step, 1), :]

    gain_copy(3, cg.at[1 - c, x], partner).wait_recv()
    for index, d in enumerate((-1, 1, 2)):
        gain_copy(4 + index, cg.at[1 - c, turn(x, d)], partner).wait_recv()
    put_split(ct_h, ct_l, ..., jnp.concatenate([cg[core, place] for place in range(4) for core in range(2)], 0))
    offsets = product(forc16[...], ct_h[...], ct_l[...]) + product(obs16[...], gain_h[...], gain_l[...], True)
    off8[...] = offsets[:8]

    def swap(index, core):
        slot = gx.at[core, index]
        return pltpu.make_async_remote_copy(
            src_ref=slot,
            dst_ref=slot,
            send_sem=send_b.at[index],
            recv_sem=recv_b.at[index],
            device_id=partner,
            device_id_type=MESH,
        )

    def put_first(ks, core, value):
        high, low = split(value)
        for spot in range(4):
            target = pl.ds(pl.multiple_of(spot * 96 + core * W, 16), W)
            b_h[2 * first.s[ks], target, :] = high[W * spot : W * (spot + 1)]
            b_l[2 * first.s[ks], target, :] = low[W * spot : W * (spot + 1)]

    def put_other(ks, core, value):
        high, low = split(value)
        target = pl.ds(pl.multiple_of(other.s[ks] * 96 + core * W, 16), W)
        for spot in range(4):
            b_h[2 * spot + 1, target, :] = high[W * spot : W * (spot + 1)]
            b_l[2 * spot + 1, target, :] = low[W * spot : W * (spot + 1)]

    def kept(row, offset):
        return jnp.where(rows_of + offset == cols_of, ret8[pl.ds(row, 1), :], 0.0)

    def step_first(ks):
        place = first.s[ks]
        raw = [ga[c, place, spot] + kept(2 * place, spot * 96 + c * W) for spot in range(4)]
        value = product(jnp.concatenate(raw, 0), ct_h[...], ct_l[...])
        gx[c, ks] = value
        put_first(ks, c, value)
        swap(ks, c).start()

    def step_other(ks):
        place = other.s[ks]
        raw = [gb[c, place, spot] + kept(2 * spot + 1, place * 96 + c * W) for spot in range(4)]
        value = product(jnp.concatenate(raw, 0), ct_h[...], ct_l[...])
        gx[c, 4 + ks] = value
        put_other(ks, c, value)
        swap(4 + ks, c).start()

    def take_first(ks):
        swap(ks, 1 - c).wait_recv()
        put_first(ks, 1 - c, gx[1 - c, ks])

    def take_other(ks):
        swap(4 + ks, 1 - c).wait_recv()
        put_other(ks, 1 - c, gx[1 - c, 4 + ks])

    def ready(gather, ks):
        for kf in range(4):
            gather.shared(kf, ks)

    step_first(0)
    first.second_near(1)
    other.second_near(1)
    step_other(0)
    first.second_near(2)
    other.second_near(2)
    take_first(0)
    first.second_near(3)
    other.second_near(3)
    step_first(1)
    first.second_far(0)
    other.second_far(0)
    step_first(2)
    first.second_far(1)
    other.second_far(1)
    step_other(1)
    first.second_far(2)
    other.second_far(2)
    step_other(2)
    take_other(0)
    take_first(1)
    take_first(2)
    take_other(1)
    first.second_far(3)
    step_first(3)
    other.second_far(3)
    step_other(3)
    take_other(2)
    take_first(3)
    take_other(3)

    row32 = lax.broadcasted_iota(jnp.int32, (32, N), 0)
    col32 = lax.broadcasted_iota(jnp.int32, (32, N), 1)
    start24 = (z * 4 + x) * CR
    walk = ((row32 < CR) & (row32 + start24 == col32)).astype(F32)
    for j in range(7, -1, -1):
        wc[j] = walk
        walk = product(walk, b_h[j], b_l[j], True)
    stage[1] = walk
    mine_a, mine_b = ea.at[c, z, x], eb.at[c, x, z]

    def ship(index, source, target, slot, device):
        return pltpu.make_async_remote_copy(
            src_ref=source,
            dst_ref=target,
            send_sem=send_y.at[index],
            recv_sem=recv_y.at[slot],
            device_id=device,
            device_id_type=MESH,
        )

    def ships(first_core, act):
        near, far = pl.ds(0, 256), pl.ds(256, 128)
        if first_core:

            @pl.when(y == 1)
            def _():
                for d in range(2):
                    act(ship(d, stage.at[1, pl.ds(0, CR)], mine_a, 2, y_to[d]))

            @pl.when(y == 2)
            def _():
                act(ship(0, stage.at[1, pl.ds(0, CR)], mine_b, 3, y_to[0]))

            return
        packed, mean = stage.at[2, pl.ds(0, CR)], stage.at[0, pl.ds(CR, 8)]

        @pl.when(y == 0)
        def _():
            for d in range(3):
                act(ship(3 * d, packed.at[:, pl.ds(0, 128)], mine_a.at[:, far], 0, y_to[d]))
                act(ship(3 * d + 1, packed.at[:, pl.ds(128, 128)], mine_b.at[:, far], 1, y_to[d]))
                act(ship(3 * d + 2, mean, near_mean.at[0], 4, y_to[d]))

        @pl.when(y == 1)
        def _():
            for d in range(2):
                act(ship(2 * d, packed.at[:, near], mine_a.at[:, near], 2, y_to[d]))
                act(ship(2 * d + 1, mean, near_mean.at[1], 5, y_to[d]))

        @pl.when(y == 2)
        def _():
            act(ship(0, packed.at[:, near], mine_b.at[:, near], 3, y_to[0]))
            act(ship(1, mean, near_mean.at[2], 6, y_to[0]))

    def pass_mean(index):
        return pltpu.make_async_remote_copy(
            src_ref=near_mean.at[index],
            dst_ref=near_mean.at[index],
            send_sem=send_m.at[index],
            recv_sem=recv_m.at[index],
            device_id=partner,
            device_id_type=MESH,
        )

    @pl.when(c == 0)
    def _():
        ships(True, lambda copy: copy.start())

    @pl.when(c == 1)
    def _():
        left = wc[...].reshape(256, N)
        spread = product(left, ct_h[...], ct_l[...], True).reshape(8, 32, N) * noise8[...].reshape(8, 1, N)
        noise = product(spread.reshape(256, N), ct_h[...], ct_l[...]) + product(left, fix_h[...], fix_l[...])
        gc[...] = noise.reshape(8, 32, N)

        @pl.when(y == 0)
        def _():
            begin = product(stage[1], p_h[...], p_l[...])
            stage[0] = jnp.where(row32 == CR, pm_v[...].reshape(1, N), begin)

        @pl.when(y != 0)
        def _():
            stage[0] = jnp.zeros((32, N), F32)

        grown = stage[0]
        for j in range(8):
            grown = product(grown, b_h[j], b_l[j])
            grown = grown + gc[j] + jnp.where(row32 == CR, off8[pl.ds(j, 1), :], 0.0)
        stage[0] = grown
        band = row32[:, :128] + start24
        low, high = band < 128, band >= 256
        one, two, three = (grown[:, 128 * b : 128 * (b + 1)] for b in range(3))
        stage[2, :, pl.ds(0, 128)] = jnp.where(low, one, jnp.where(high, three, two))
        stage[2, :, pl.ds(128, 128)] = jnp.where(low, two, jnp.where(high, one, three))
        ships(False, lambda copy: copy.start())

    last = 2 * z + 1
    wf[last, pl.ds(W, W), :] = eye_rows
    behind = product(eye_rows, b_h[last], b_l[last], True)
    w0_s[pl.ds(0, W), :] = eye_rows
    w0_s[pl.ds(W, W), :] = behind

    @pl.loop(0, 2 * z + 1)
    def _(i):
        j = 2 * z - i
        rows = w0_s[...]
        wf[j] = rows
        w0_s[...] = product(rows, b_h[j], b_l[j], True)

    def noise_rows(part):
        span = pl.ds(4 * part, 4)
        rows = wf[span].reshape(N, N)
        wide = product(rows, ct_h[...], ct_l[...], True).reshape(4, 96, N)
        wide = wide * noise8[pl.ds(4 * part, 4), :].reshape(4, 1, N)
        value = product(wide.reshape(N, N), ct_h[...], ct_l[...]) + product(rows, fix_h[...], fix_l[...])
        gf[span] = value.reshape(4, 96, N)


    @pl.when((c == 0) & (y >= 2))
    def _():
        ship(0, mine_a, mine_a, 2, partner).wait_recv()

    @pl.when((c == 0) & (y >= 3))
    def _():
        ship(0, mine_b, mine_b, 3, partner).wait_recv()

    @pl.when((c == 1) & (y >= 1))
    def _():
        ship(0, mine_a.at[:, pl.ds(256, 128)], mine_a.at[:, pl.ds(256, 128)], 0, partner).wait_recv()
        ship(0, mine_b.at[:, pl.ds(256, 128)], mine_b.at[:, pl.ds(256, 128)], 1, partner).wait_recv()

    @pl.when((c == 1) & (y >= 2))
    def _():
        ship(0, mine_a.at[:, pl.ds(0, 256)], mine_a.at[:, pl.ds(0, 256)], 2, partner).wait_recv()

    @pl.when((c == 1) & (y >= 3))
    def _():
        ship(0, mine_b.at[:, pl.ds(0, 256)], mine_b.at[:, pl.ds(0, 256)], 3, partner).wait_recv()

    third = PlaneGather(lambda core, f, s: ea.at[core, s, f], CR, c, x, z, x_to, z_to, partner, send3, recv3, 0, sent, STRAIGHT3)
    fourth = PlaneGather(
        lambda core, f, s: eb.at[core, s, f], CR, c, z, x, z_to, x_to, partner, send3, recv3, PER_CLASS, sent, STRAIGHT3
    )
    for gather in (third, fourth):
        gather.first_own(gather.at(0, 0))
    for gather in (third, fourth):
        gather.first_own_far(gather.at(0, 0))
    for gather in (third, fourth):
        gather.second(0)
        gather.share(0, 0)

    for plane in range(3):

        @pl.when((c == 1) & (y > plane))
        def _():
            ship(0, near_mean.at[plane], near_mean.at[plane], 4 + plane, partner).wait_recv()
            pass_mean(plane).start()

    own_half = pl.ds(pl.multiple_of(c * 192, 64), 192)
    ph_f[c] = b_h[0, own_half, :].astype(F32) + b_l[0, own_half, :].astype(F32)

    @pl.loop(1, 2 * z + 1)
    def _(j):
        ph_f[c] = product(ph_f[c], b_h[j], b_l[j])

    def swap_phi(core):
        slot = ph_f.at[core]
        return pltpu.make_async_remote_copy(
            src_ref=slot,
            dst_ref=slot,
            send_sem=send_b.at[8],
            recv_sem=recv_b.at[8],
            device_id=partner,
            device_id_type=MESH,
        )

    third.first_near()
    fourth.first_near()
    third.first_far()
    fourth.first_far()
    swap_phi(c).start()
    noise_rows(0)

    third.second_near(0)
    fourth.second_near(0)

    @pl.when(z >= 2)
    def _():
        noise_rows(1)

    for kf in (1, 2):
        third.second_near(kf)
        fourth.second_near(kf)

    row16 = lax.broadcasted_iota(jnp.int32, (16, N), 0)

    def mean_rows(row):
        return jnp.where(row16 == 0, row, 0.0)

    def fresh(j):
        return jnp.concatenate([gf[j], mean_rows(off8[pl.ds(j, 1), :])], 0)

    nz[...] = fresh(0)

    @pl.loop(1, z + 1)
    def _(j):
        nz[...] = product(nz[...], b_h[j], b_l[j]) + fresh(j)

    third.second_near(3)
    fourth.second_near(3)

    @pl.loop(z + 1, 2 * z + 1)
    def _(j):
        nz[...] = product(nz[...], b_h[j], b_l[j]) + fresh(j)

    swap_phi(1 - c).wait_recv()
    for core in range(2):
        high, low = split(ph_f[core])
        ph_h[pl.ds(192 * core, 192), :] = high
        ph_l[pl.ds(192 * core, 192), :] = low

    spots = [(a, b) for a in range(4) for b in range(4)]

    def symmetric(own, after):
        d0, d1, d2 = (own[128 * b : 128 * (b + 1)] for b in range(3))
        u0, u1, u2 = (after[128 * b : 128 * (b + 1)] for b in range(3))
        rows = ((d0, u0, u2.T), (u0.T, d1, u1), (u2, u1.T, d2))
        return jnp.concatenate([jnp.concatenate(row, 1) for row in rows], 0)

    def columns(pick, block):
        return jnp.concatenate([pick(a, b)[:, 128 * block : 128 * (block + 1)] for a, b in spots], 0)

    def from_a(a, b):
        return ea[1, a, b]

    def from_b(a, b):
        return eb[1, b, a]

    def ready_all():
        for ks in range(4):
            ready(third, ks)
            ready(fourth, ks)

    def prepare_steps():
        @pl.when(y == 3)
        def _():
            put_split(t2_h, t2_l, ..., jnp.concatenate([eb[0, b, a] for a, b in spots], 0))
            v2_s[...] = product(w0_s[...], t2_h[...], t2_l[...])

        @pl.when(y != 3)
        def _():
            v2_s[...] = w0_s[...]

        @pl.when(y >= 2)
        def _():
            put_split(t1_h, t1_l, ..., jnp.concatenate([ea[0, a, b] for a, b in spots], 0))
            v1_s[...] = product(v2_s[...], t1_h[...], t1_l[...])

        @pl.when(y < 2)
        def _():
            v1_s[...] = v2_s[...]

    for kf in range(4):
        third.second_far(kf)
        fourth.second_far(kf)

    @pl.when(c == 0)
    def _():
        prepare_steps()
        ready_all()

    @pl.when(c == 1)
    def _():
        ready_all()
        prepare_steps()

    for plane in range(3):

        @pl.when((c == 0) & (y > plane))
        def _():
            pass_mean(plane).wait_recv()

    def covariance_before():
        return split(symmetric(columns(from_a, 2), columns(from_b, 2)))

    def mean_of(plane):
        return mean_rows(near_mean[plane, pl.ds(0, 1), :])

    def joined(rows, row):
        return jnp.concatenate([rows, row], 0)

    @pl.when(y == 0)
    def _():
        xs[...] = joined(product(v1_s[...], p_h[...], p_l[...]), mean_rows(pm_v[...].reshape(1, N)))

    @pl.when(y == 1)
    def _():
        xs[...] = joined(product(v1_s[...], *covariance_before()), mean_of(0))

    @pl.when(y >= 2)
    def _():
        value = joined(product(v1_s[...], *covariance_before()), mean_of(0))
        added = product(v2_s[...], *split(symmetric(columns(from_a, 0), columns(from_a, 1))))
        xs[...] = product(value, t1_h[...], t1_l[...], True) + joined(added, mean_of(1))

    @pl.when(y >= 3)
    def _():
        added = product(w0_s[...], *split(symmetric(columns(from_b, 0), columns(from_b, 1))))
        xs[...] = product(xs[...], t2_h[...], t2_l[...], True) + joined(added, mean_of(2))

    xs[...] = product(xs[...], ph_h[...], ph_l[...]) + nz[...]

    covariances[0] = xs[pl.ds(0, W), :]
    means[pl.ds(0, 1), :] = xs[pl.ds(96, 1), :]
    value = product(xs[pl.ds(W, 64), :], b_h[last], b_l[last])
    covariances[1] = value[:W] + gf[last, pl.ds(W, W), :]
    means[pl.ds(1, 1), :] = value[W : W + 1] + off8[pl.ds(last, 1), :]
    drain()


def finish(near_means, near_covariances, means, covariances, done):
    copies = [
        pltpu.make_async_copy(near_means, means, done.at[0]),
        pltpu.make_async_copy(near_covariances, covariances, done.at[1]),
    ]
    for copy in copies:
        copy.start()
    for copy in copies:
        copy.wait()


def vmem(shape, dtype=F32):
    return pltpu.VMEM(shape, dtype)


def pair(shape):
    return [vmem(shape, BF16), vmem(shape, BF16)]


def per_device(mixing, retention, forcing, observations, model_noise, obs_noise, gain, obs_t, prior_mean, prior_factor):
    dma = pltpu.SemaphoreType.DMA
    square = (N, N)
    near = pl.pallas_call(
        kernel,
        out_shape=(pltpu.VMEM((2, N), F32), pltpu.VMEM((2, W, N), F32)),
        in_specs=[pl.BlockSpec(memory_space=pltpu.HBM)] * 10,
        out_specs=(pl.BlockSpec(memory_space=pltpu.VMEM),) * 2,
        scratch_shapes=[
            vmem((2, 4, 4, W, N)),
            vmem((2, 4, 4, W, N)),
            vmem((2, 8, 4 * W, N)),
            vmem((2, 4, W, N)),
            vmem((2, 4, 4, CR, N)),
            vmem((2, 4, 4, CR, N)),
            vmem((4, 2, N)),
            vmem((4, 2, N)),
            vmem((4, 2, NOBS)),
            vmem((4, 2, N)),
            vmem((8, N)),
            vmem((16, N)),
            vmem((16, NOBS)),
            vmem((8, N)),
            vmem((1, NOBS)),
            vmem((N, NOBS)),
            *pair((N, NOBS)),
            vmem((W, NOBS)),
            vmem((N,)),
            vmem(square),
            *pair(square),
            *pair(square),
            *pair(square),
            *pair((8, N, N)),
            vmem((8, N)),
            vmem((8, 32, N)),
            vmem((8, 32, N)),
            vmem((8, 96, N)),
            vmem((8, 96, N)),
            vmem((3, 32, N)),
            vmem((3, 8, N)),
            *pair(square),
            *pair(square),
            *pair(square),
            *pair(square),
            vmem((96, N)),
            vmem((96, N)),
            vmem((96, N)),
            vmem((112, N)),
            vmem((112, N)),
            vmem((2, 192, N)),
            *pair(square),
            dma((2 * PER_CLASS,)),
            dma((2 * PER_CLASS,)),
            dma((2 * PER_CLASS,)),
            dma((2 * PER_CLASS,)),
            dma((7,)),
            dma((7,)),
            dma((9,)),
            dma((9,)),
            dma((12,)),
            dma((12,)),
            dma((9,)),
            dma((7,)),
            dma((3,)),
            dma((3,)),
            dma((9,)),
            dma((9,)),
            dma((11,)),
        ],
        compiler_params=pltpu.CompilerParams(
            collective_id=0, has_side_effects=True, vmem_limit_bytes=60 * 1024 * 1024
        ),
        name="prefix",
    )(
        mixing, retention, forcing, observations, model_noise, obs_noise.reshape(1, NOBS), gain, obs_t,
        prior_mean, prior_factor,
    )
    return pl.pallas_call(
        finish,
        out_shape=(jax.ShapeDtypeStruct((2, N), F32), jax.ShapeDtypeStruct((2, W, N), F32)),
        in_specs=[pl.BlockSpec(memory_space=pltpu.VMEM)] * 2,
        out_specs=(pl.BlockSpec(memory_space=pltpu.HBM),) * 2,
        scratch_shapes=[pltpu.SemaphoreType.DMA((2,))],
        compiler_params=pltpu.CompilerParams(vmem_limit_bytes=1024 * 1024),
        name="finish",
    )(*near)


def solution(mesh):
    grid = Mesh(mesh.devices.reshape(4, 4, 4, 2), SEG + COL)
    placed = (
        P(SEG, COL, None),
        P(SEG, None),
        P(SEG, None),
        P(SEG, None),
        P(SEG, None),
        P(),
        P(),
        P(COL, None),
        P(),
        P(),
    )
    return jax.shard_map(
        per_device,
        mesh=grid,
        in_specs=placed,
        out_specs=(P(SEG, None), P(SEG, COL, None)),
        check_vma=False,
    )
```
